256 devices in a mesh: dp: 64 (over y_lo, z, x), cluster: 4 (over y_hi, core).
Axes of the slice: x: 4, y: 4 (y_hi: 2, y_lo: 2; y = y_hi * 2 + y_lo), z: 8, core: 2. Of those that a mesh axis runs over, the one named last changes fastest.
Arguments:
- home_rows: bfloat16 [393216, 768], P(('dp', 'cluster')), may hold values from -6 to 6
- guest_rows: bfloat16 [65536, 768], P(('dp', 'cluster')), may hold values from -6 to 6
- home_cluster: int32 [1536], replicated, may hold values from 0 to 7, as said below
- guest_cluster: int32 [256], replicated, may hold values from 0 to 7, as said below
- pair_mask: int32 [256, 6, 64], P(('dp', 'cluster')), may hold values from 0 to 1, as said below
Outputs:
- home_score: float32 [393216], P(('dp', 'cluster'))
- guest_score: float32 [65536], P(('dp', 'cluster'))
The draws below stay inside these ranges and needn't reach their ends.
Inputs may be any that keep to these rules, and one draw needn't show every extreme that they name: `home_cluster`: blocks of the devices at cluster indices 2 g and 2 g + 1 carry ids from g * 4 to (g + 1) * 4 - 1. `guest_cluster`: blocks of the devices at cluster indices 2 g and 2 g + 1 carry ids from g * 4 to (g + 1) * 4 - 1. `pair_mask`: an entry is 1 where the resident block and the visiting block it names carry one cluster id, else 0.
All inputs are finite; a program needn't handle non-finite values.
Results may differ from the reference program's by a relative error of at most 0.0003.
Values may be sent and summed in bfloat16 or wider, within the bound.
No kernel may reach another device: no remote copies, remote signals or barrier semaphores. Data moves between devices by JAX's collectives and lax.ppermute only.
A program may use at most 128 MiB of HBM per device.

```python
import jax
import jax.numpy as jnp
import numpy as np
from jax import lax

D = 768
BLOCK = 256
STAT_DEV = 6
CLUSTERS = 4
STAT_ROWS = 393216
GUEST_ROWS = 65536
N_DP = 64
N_CLUSTER = 4


def cluster_tables(key):
    key_home = jax.random.fold_in(key, 11)
    key_guest = jax.random.fold_in(key, 12)
    key_label = jax.random.fold_in(key, 13)
    devices_all = N_DP * N_CLUSTER
    weights = [1000 // (i + 1) for i in range(CLUSTERS)]
    bounds = np.cumsum(np.array(weights, dtype=np.int64))
    overall = int(bounds[-1])
    inner = jnp.asarray(bounds[:-1].astype(np.int32))
    relabel = jax.random.permutation(key_label, CLUSTERS).astype(jnp.int32)
    groups = jnp.arange(devices_all, dtype=jnp.int32) % N_CLUSTER // 2

    def pick_ids(which, slots):
        drawn = jax.random.randint(which, (devices_all, slots), 0, overall, dtype=jnp.int32)
        picked = jnp.sum((drawn[..., None] >= inner).astype(jnp.int32), axis=-1)
        return groups[:, None] * CLUSTERS + relabel[picked]
    home_ids = pick_ids(key_home, STAT_DEV)
    guest_ids = pick_ids(key_guest, 1)[:, 0]
    home_grid = home_ids.reshape(N_DP, N_CLUSTER, STAT_DEV)
    guest_grid = guest_ids.reshape(N_DP, N_CLUSTER)
    mirrored = guest_grid[:, jnp.bitwise_xor(jnp.arange(N_CLUSTER, dtype=jnp.int32), 1)]
    matched = (home_grid[:, :, :, None] == jnp.transpose(mirrored)[None, :, None, :]).astype(jnp.int32)
    return (home_ids.reshape(-1), guest_ids, matched.reshape(devices_all, STAT_DEV, N_DP))


def draw_home_cluster(key, part):
    return cluster_tables(key)[0]


def draw_guest_cluster(key, part):
    return cluster_tables(key)[1]


def draw_pair_mask(key, part):
    return cluster_tables(key)[2]


def block_levels(own_key, extent, shards, low, largest):
    def one(position, blocks):
        steps = jax.random.uniform(jax.random.fold_in(jax.random.fold_in(own_key, 6), position), (blocks,), jnp.float32, low / len(shards), largest / len(shards))
        return jnp.repeat(jnp.exp(steps), extent[position] // blocks).reshape((-1,) + (1,) * (len(extent) - position - 1))

    gain = one(*shards[0])
    for cut in shards[1:]:
        gain = gain * one(*cut)
    return gain


def bell_draw(stream_key, shape, spread, bound, split=(), kind=jnp.bfloat16):
    result = jax.random.normal(stream_key, shape, jnp.float32) * spread
    if len(split) > 0:
        result = block_levels(stream_key, shape, split, -0.22, 0.18) * result
    return jnp.clip(result, min=-bound, max=bound).astype(kind)


def setup_inputs(seed: int = 0) -> dict:
    arg_keys = jax.random.split(jax.random.key(seed), 6)
    home_rows = bell_draw(arg_keys[0], (STAT_ROWS, D), 1.0, 6.0, ((0, 256),))
    guest_rows = bell_draw(arg_keys[1], (GUEST_ROWS, D), 1.0, 6.0, ((0, 256),))
    home_cluster = draw_home_cluster(jax.random.fold_in(arg_keys[5], 71), 0)
    guest_cluster = draw_guest_cluster(jax.random.fold_in(arg_keys[5], 71), 0)
    pair_mask = draw_pair_mask(jax.random.fold_in(arg_keys[5], 71), 0)
    return {"home_rows": home_rows, "guest_rows": guest_rows, "home_cluster": home_cluster, "guest_cluster": guest_cluster, "pair_mask": pair_mask}


SHARPNESS = 30.0
EPSILON = 1e-06

def reference(home_rows, guest_rows, home_cluster, guest_cluster, pair_mask):
    devices_all = N_DP * N_CLUSTER
    resident = home_rows.reshape(devices_all * STAT_DEV, BLOCK, D)
    visiting = guest_rows.reshape(N_DP, N_CLUSTER, BLOCK, D)
    res_f = resident.astype(jnp.float32)
    inv_resident = 1.0 / jnp.sqrt(lax.optimization_barrier(jnp.sum(res_f * res_f, axis=-1)) + EPSILON)
    vis_f = visiting.astype(jnp.float32)
    inv_visiting = 1.0 / jnp.sqrt(lax.optimization_barrier(jnp.sum(vis_f * vis_f, axis=-1)) + EPSILON)
    listed_all = pair_mask.reshape(devices_all * STAT_DEV, N_DP).astype(jnp.float32)

    def one_block(guest_acc, number):
        device = number // STAT_DEV
        column = device % N_CLUSTER
        partner = jnp.bitwise_xor(column, 1).astype(jnp.int32)
        partners = lax.dynamic_index_in_dim(visiting, partner, 1, keepdims=False).reshape(N_DP * BLOCK, D)
        inv_partner = lax.dynamic_index_in_dim(inv_visiting, partner, 1, keepdims=False).reshape(N_DP * BLOCK)
        block_rows = resident[number]
        products = jnp.dot(block_rows, partners.T, preferred_element_type=jnp.float32)
        cosine = products * inv_resident[number][:, None] * inv_partner[None, :]
        weights = jnp.repeat(listed_all[number], BLOCK)
        kernel_tile = jnp.exp(SHARPNESS * cosine) * weights[None, :]
        row_part = lax.optimization_barrier(jnp.sum(kernel_tile, axis=1))
        col_part = lax.optimization_barrier(jnp.sum(kernel_tile, axis=0)).reshape(N_DP, BLOCK)
        guest_acc = guest_acc.at[:, partner].add(col_part)
        return (guest_acc, row_part)
    start_acc = jnp.zeros((N_DP, N_CLUSTER, BLOCK), jnp.float32)
    guest_acc, home_density = lax.scan(one_block, start_acc, jnp.arange(devices_all * STAT_DEV, dtype=jnp.int32))
    id_range = jnp.arange(N_CLUSTER // 2 * CLUSTERS, dtype=jnp.int32)
    members = lax.optimization_barrier(jnp.sum((home_cluster[:, None] == id_range[None, :]).astype(jnp.int32), axis=0))
    members = members + lax.optimization_barrier(jnp.sum((guest_cluster[:, None] == id_range[None, :]).astype(jnp.int32), axis=0))
    home_members = jnp.take(members, home_cluster).astype(jnp.float32)
    guest_members = jnp.take(members, guest_cluster).astype(jnp.float32)
    home_score = jnp.log(1.0 + home_density) - jnp.log(home_members)[:, None]
    guest_density = guest_acc.reshape(devices_all, BLOCK)
    guest_score = jnp.log(1.0 + guest_density) - jnp.log(guest_members)[:, None]
    return (home_score.reshape(-1), guest_score.reshape(-1))
```

```python
import functools
import math

import jax
import jax.numpy as jnp
from jax import lax
from jax.experimental import pallas as pl
from jax.experimental.pallas import tpu as pltpu
from jax.sharding import Mesh
from jax.sharding import PartitionSpec as P

BLOCK = 256
LANES = 128
SHARPNESS = 30.0
EPSILON = 1e-06
EXP2_SCALE = SHARPNESS / math.log(2.0)

NY, NZ, NX, NH, NK = 2, 8, 4, 2, 2
AXES = ("y", "z", "x", "h", "k")

SLOTS = (
    ((-1, 0), (0, 0)), ((0, 1), (0, 0)), ((1, 0), (0, 0)), ((0, -1), (0, 0)),
), (
    ((0, 1), (-1, 0)), ((0, -1), (-1, 0)), ((1, 0), (1, 0)), ((-1, 0), (-1, 0)),
), (
    ((1, 0), (2, 0)), ((-1, 0), (-1, -1)), ((0, 1), (-1, 1)), ((0, -1), (2, 0)),
), (
    ((-1, 0), (-2, -1)), ((0, 1), (0, 1)), ((1, 0), (0, 1)), ((0, -1), (1, 0)),
), (
    ((1, 0), (1, 1)), ((-1, 0), (-1, 1)), ((0, -1), (1, -1)), ((0, 1), (3, 0)),
), (
    ((1, 0), (1, 2)), ((0, 1), (-3, -1)), ((0, -1), (-3, -1)), ((-1, 0), (-1, 2)),
), (
    ((0, 1), (-3, 0)), ((0, -1), (3, 0)), ((1, 0), (3, 0)), ((-1, 0), (-3, 2)),
), (
    ((-1, 0), (4, 2)), ((0, -1), (4, 2)), ((1, 0), (3, -1)),
)


def node(dz, dx):
    return ((dz + 3) % NZ - 3, (dx + 1) % NX - 1)


def shift(value, dz, dx):
    if dx == 0:
        return lax.ppermute(value, "z", [(i, (i + dz) % NZ) for i in range(NZ)])
    if dz == 0:
        return lax.ppermute(value, "x", [(i, (i + dx) % NX) for i in range(NX)])
    return lax.ppermute(
        value,
        ("z", "x"),
        [(z * NX + x, (z + dz) % NZ * NX + (x + dx) % NX) for z in range(NZ) for x in range(NX)],
    )


def to_sibling(value):
    return lax.ppermute(value, "k", [(0, 1), (1, 0)])


def to_partner(value):
    return lax.ppermute(value, ("y", "k"), [(0, 3), (1, 2), (2, 1), (3, 0)])


def inverse_norms(rows):
    values = rows.astype(jnp.float32)
    return 1.0 / jnp.sqrt(jnp.sum(values * values, axis=-1) + EPSILON)


def pair_kernel(n_guest, n_sets, guest_ids, *refs):
    set_ids, refs = refs[:n_sets], refs[n_sets:]
    guests, refs = refs[:n_guest], refs[n_guest:]
    guest_scale, refs = refs[0], refs[1:]
    sets, refs = refs[:n_sets], refs[n_sets:]
    scales, refs = refs[:n_sets], refs[n_sets:]
    rows_in, refs = refs[:n_sets], refs[n_sets:]
    rows_out, refs = refs[:n_sets], refs[n_sets:]
    cols_out, cols = refs
    cols[...] = jnp.zeros_like(cols)
    for ids, blocks, scale, before, after in zip(set_ids, sets, scales, rows_in, rows_out, strict=True):

        @pl.loop(0, blocks.shape[0])
        def _(r, ids=ids, blocks=blocks, scale=scale, before=before, after=after):
            total = before[r]
            for g in range(n_guest):
                keep = jnp.where(ids[r] == guest_ids[g], 1.0, 0.0)
                products = lax.dot_general(
                    blocks[r], guests[g][...], (((1,), (1,)), ((), ())), preferred_element_type=jnp.float32
                )
                for half in range(BLOCK // LANES):
                    lanes = slice(half * LANES, (half + 1) * LANES)
                    tile = jnp.exp2(products[:, lanes] * scale[r] * guest_scale[g : g + 1, lanes]) * keep
                    total = total + tile
                    cols[g, :, lanes] += jnp.sum(tile.reshape(BLOCK // 8, 8, LANES), axis=0)
            after[r] = total

    for g in range(n_guest):
        cols_out[g : g + 1, :] = jnp.sum(cols[g], axis=0, keepdims=True)


def pairs(guests, sets, rows):
    n_guest, n_sets = len(guests), len(sets)
    smem = pl.BlockSpec(memory_space=pltpu.SMEM)
    vmem = pl.BlockSpec(memory_space=pltpu.VMEM)
    tiles = n_guest * sum(s[0].shape[0] for s in sets)
    first_row = 1 + n_sets + n_guest + 1 + 2 * n_sets
    outs = pl.pallas_call(
        functools.partial(pair_kernel, n_guest, n_sets),
        in_specs=[smem] * (1 + n_sets) + [vmem] * (n_guest + 1 + 3 * n_sets),
        out_specs=[vmem] * (n_sets + 1),
        out_shape=[jax.ShapeDtypeStruct(r.shape, jnp.float32) for r in rows]
        + [jax.ShapeDtypeStruct((n_guest, BLOCK), jnp.float32)],
        scratch_shapes=[pltpu.VMEM((n_guest, 8, BLOCK), jnp.float32)],
        input_output_aliases={first_row + j: j for j in range(n_sets)},
        compiler_params=pltpu.CompilerParams(vmem_limit_bytes=40 << 20),
        cost_estimate=pl.CostEstimate(
            flops=tiles * 2 * BLOCK * BLOCK * 768, bytes_accessed=tiles * 400000, transcendentals=tiles * BLOCK * BLOCK
        ),
        name="pairs",
    )(
        jnp.stack([g[2] for g in guests]),
        *[s[2] for s in sets],
        *[g[0] for g in guests],
        jnp.stack([g[1] for g in guests]),
        *[s[0] for s in sets],
        *[s[1] for s in sets],
        *rows,
    )
    return list(outs[:n_sets]), outs[n_sets]


def body(home_rows, guest_rows, home_cluster, guest_cluster, pair_mask):
    slots = home_rows.shape[0] // BLOCK
    y, z, x, h, k = (lax.axis_index(a) for a in AXES)
    ids_home = home_cluster.reshape(NY, NZ, NX, NH, NK, slots)
    ids_guest = guest_cluster.reshape(NY, NZ, NX, NH, NK)

    def resident_set(blocks, yy):
        blocks = blocks.reshape(slots, BLOCK, -1)
        scale = jnp.broadcast_to((inverse_norms(blocks) * EXP2_SCALE)[..., None], (slots, BLOCK, LANES))
        return blocks, scale, ids_home[yy, z, x, h, 1 - k]

    near = resident_set(to_sibling(home_rows), y)
    far = resident_set(to_partner(home_rows), 1 - y)
    near_rows = jnp.zeros((slots, BLOCK, LANES), jnp.float32)
    far_rows = jnp.zeros((slots, BLOCK, LANES), jnp.float32)

    held = {(0, 0): guest_rows}

    def guest(n):
        return held[n], inverse_norms(held[n]), ids_guest[y, (z - n[0]) % NZ, (x - n[1]) % NX, h, k]

    col_parts = {}

    def note(nodes, cols):
        for i, n in enumerate(nodes):
            col_parts.setdefault(n, []).append(cols[i])

    early = []
    late_from = 4
    for s, slot in enumerate(SLOTS):
        arrived = []
        for (dz, dx), parent in slot:
            child = node(parent[0] + dz, parent[1] + dx)
            held[child] = shift(held[parent], dz, dx)
            arrived.append(child)
        if s == 0:
            arrived = [(0, 0), *arrived]
        if s < late_from:
            (near_rows,), cols = pairs([guest(n) for n in arrived], [near], [near_rows])
            early += arrived
        else:
            if s == late_from:
                (far_rows,), cols = pairs([guest(n) for n in early], [far], [far_rows])
                note(early, cols)
            (near_rows, far_rows), cols = pairs([guest(n) for n in arrived], [near, far], [near_rows, far_rows])
        note(arrived, cols)

    order = [node(dz, dx) for dz in range(NZ) for dx in range(NX)]
    by_node = jnp.stack([functools.reduce(jnp.add, col_parts[n]) for n in order]).reshape(NZ, NX, BLOCK)
    source_z = (z - jnp.arange(NZ)) % NZ
    source_x = (x - jnp.arange(NX)) % NX
    outgoing = by_node[source_z][:, source_x].reshape(NZ * NX, BLOCK)
    incoming = lax.all_to_all(outgoing, ("z", "x"), 0, 0, tiled=True)
    guest_density = jnp.sum(incoming, axis=0)
    home_density = to_sibling(jnp.sum(near_rows, axis=-1)) + to_partner(jnp.sum(far_rows, axis=-1))

    home_ids = ids_home[y, z, x, h, k]
    guest_id = ids_guest[y, z, x, h, k]

    def members(ids):
        count = jnp.sum((home_cluster[None, :] == ids[:, None]).astype(jnp.int32), axis=1)
        count = count + jnp.sum((guest_cluster[None, :] == ids[:, None]).astype(jnp.int32), axis=1)
        return count.astype(jnp.float32)

    home_score = jnp.log(1.0 + home_density) - jnp.log(members(home_ids))[:, None]
    guest_score = jnp.log(1.0 + guest_density) - jnp.log(members(guest_id[None]))
    return home_score.reshape(-1), guest_score


def solution(mesh):
    whole = Mesh(mesh.devices.reshape(NY, NZ, NX, NH, NK), AXES)
    placed = (P(AXES, None), P(AXES, None), P(), P(), P(AXES, None, None))
    return jax.shard_map(
        body, mesh=whole, in_specs=placed, out_specs=(P(AXES), P(AXES)), check_vma=False
    )
```

```python
import functools
import math

import jax
import jax.numpy as jnp
from jax import lax
from jax.experimental import pallas as pl
from jax.experimental.pallas import tpu as pltpu
from jax.sharding import Mesh
from jax.sharding import PartitionSpec as P

BLOCK = 256
LANES = 128
SHARPNESS = 30.0
EPSILON = 1e-06
EXP2_SCALE = SHARPNESS / math.log(2.0)
UNROLL = 4
FAR_FROM = 5
IDS_AT = 3

NY, NZ, NX, NH, NK = 2, 8, 4, 2, 2
AXES = ("y", "z", "x", "h", "k")

SLOTS = (
    ((-1, 0), (0, 0)), ((0, 1), (0, 0)), ((1, 0), (0, 0)), ((0, -1), (0, 0)),
), (
    ((0, 1), (-1, 0)), ((0, -1), (-1, 0)), ((1, 0), (1, 0)), ((-1, 0), (-1, 0)),
), (
    ((1, 0), (2, 0)), ((-1, 0), (-1, -1)), ((0, 1), (-1, 1)), ((0, -1), (2, 0)),
), (
    ((-1, 0), (-2, -1)), ((0, 1), (0, 1)), ((1, 0), (0, 1)), ((0, -1), (1, 0)),
), (
    ((1, 0), (1, 1)), ((-1, 0), (-1, 1)), ((0, -1), (1, -1)), ((0, 1), (3, 0)),
), (
    ((1, 0), (1, 2)), ((0, 1), (-3, -1)), ((0, -1), (-3, -1)), ((-1, 0), (-1, 2)),
), (
    ((0, 1), (-3, 0)), ((0, -1), (3, 0)), ((1, 0), (3, 0)), ((-1, 0), (-3, 2)),
), (
    ((-1, 0), (4, 2)), ((0, -1), (4, 2)), ((1, 0), (3, -1)),
)


def node(dz, dx):
    return ((dz + 3) % NZ - 3, (dx + 1) % NX - 1)


def shift(value, dz, dx):
    if dx == 0:
        return lax.ppermute(value, "z", [(i, (i + dz) % NZ) for i in range(NZ)])
    if dz == 0:
        return lax.ppermute(value, "x", [(i, (i + dx) % NX) for i in range(NX)])
    return lax.ppermute(
        value,
        ("z", "x"),
        [(z * NX + x, (z + dz) % NZ * NX + (x + dx) % NX) for z in range(NZ) for x in range(NX)],
    )


def to_sibling(value):
    return lax.ppermute(value, "k", [(0, 1), (1, 0)])


def to_partner(value):
    return lax.ppermute(value, ("y", "k"), [(0, 3), (1, 2), (2, 1), (3, 0)])


def inverse_norms(rows):
    values = rows.astype(jnp.float32)
    return 1.0 / jnp.sqrt(jnp.sum(values * values, axis=-1) + EPSILON)


def lane_sums(values):
    high = values.astype(jnp.bfloat16)
    rest = values - high.astype(jnp.float32)
    middle = rest.astype(jnp.bfloat16)
    low = (rest - middle.astype(jnp.float32)).astype(jnp.bfloat16)
    terms = jnp.concatenate([high, middle, low], axis=1)
    ones = jnp.ones((8, terms.shape[1]), jnp.bfloat16)
    return lax.dot_general(ones, terms, (((1,), (1,)), ((), ())), preferred_element_type=jnp.float32)[:1]


def pair_kernel(n_guest, new_guests, table, guest_at, set_at, *refs):
    guests, refs = refs[:n_guest], refs[n_guest:]
    scale_in, refs = (None, refs) if new_guests else (refs[0], refs[1:])
    blocks, scale, rows_in, rows, cols_out, refs = *refs[:5], refs[5:]
    if new_guests:
        guest_scale, refs = refs[0], refs[1:]
    else:
        guest_scale = scale_in
    held, cols, listed, sems = refs
    n_set = blocks.shape[0]
    copies = [pltpu.make_async_copy(guests[g], held.at[g], sems.at[g]) for g in range(n_guest)]
    for copy in copies:
        copy.start()

    def list_guest(g, count):
        def list_pair(r, count):
            listed[0, count] = r
            listed[1, count] = g
            return count + jnp.where(table[set_at[0] + r] == table[guest_at[g]], 1, 0)

        return lax.fori_loop(0, n_set, list_pair, count)

    count = lax.fori_loop(0, n_guest, list_guest, 0)
    for u in range(UNROLL):
        listed[0, count + u] = 0
        listed[1, count + u] = 0
    cols[...] = jnp.zeros_like(cols)
    rows[...] = rows_in[...]
    for copy in copies:
        copy.wait()
    if new_guests:
        for g in range(n_guest):
            squares = jnp.zeros((BLOCK, LANES), jnp.float32)
            for part in range(held.shape[2] // LANES):
                values = held[g, :, part * LANES : (part + 1) * LANES].astype(jnp.float32)
                squares = squares + values * values
            guest_scale[g : g + 1, :] = 1.0 / jnp.sqrt(lane_sums(squares) + EPSILON)

    @pl.loop(0, lax.div(count + UNROLL - 1, UNROLL))
    def _(step):
        for u in range(UNROLL):
            at = step * UNROLL + u
            r, g = listed[0, at], listed[1, at]
            keep = jnp.where(at < count, 1.0, 0.0)
            products = lax.dot_general(
                blocks[r], held[g], (((1,), (1,)), ((), ())), preferred_element_type=jnp.float32
            )
            column_scale = guest_scale[pl.ds(g, 1), :]
            total = rows[r]
            for half in range(BLOCK // LANES):
                lanes = slice(half * LANES, (half + 1) * LANES)
                tile = jnp.exp2(products[:, lanes] * scale[r] * column_scale[:, lanes]) * keep
                total = total + tile
                cols[g, :, lanes] += jnp.sum(tile.reshape(BLOCK // 8, 8, LANES), axis=0)
            rows[r] = total

    for g in range(n_guest):
        cols_out[g : g + 1, :] = jnp.sum(cols[g], axis=0, keepdims=True)


def pairs(table, guest_at, set_at, guests, guest_scale, blocks, scale, rows):
    n_guest, n_set = len(guests), blocks.shape[0]
    smem = pl.BlockSpec(memory_space=pltpu.SMEM)
    vmem = pl.BlockSpec(memory_space=pltpu.VMEM)
    new = guest_scale is None
    tiles = n_guest * n_set // 3
    row = jax.ShapeDtypeStruct((n_guest, BLOCK), jnp.float32)
    outs = pl.pallas_call(
        functools.partial(pair_kernel, n_guest, new),
        in_specs=[smem] * 3 + [pl.BlockSpec(memory_space=pl.ANY)] * n_guest + [vmem] * (3 if new else 4),
        out_specs=[vmem] * (3 if new else 2),
        out_shape=[jax.ShapeDtypeStruct(rows.shape, jnp.float32), row] + [row] * new,
        scratch_shapes=[
            pltpu.VMEM((n_guest, *guests[0].shape), jnp.bfloat16),
            pltpu.VMEM((n_guest, 8, BLOCK), jnp.float32),
            pltpu.SMEM((2, n_guest * n_set + UNROLL), jnp.int32),
            pltpu.SemaphoreType.DMA((n_guest,)),
        ],
        input_output_aliases={3 + n_guest + (2 if new else 3): 0},
        compiler_params=pltpu.CompilerParams(vmem_limit_bytes=24 << 20),
        cost_estimate=pl.CostEstimate(
            flops=tiles * 4 * BLOCK * BLOCK * 768, bytes_accessed=tiles * 400000, transcendentals=tiles * BLOCK * BLOCK
        ),
        name="pairs",
    )(table, guest_at, set_at, *guests, *([] if new else [guest_scale]), blocks, scale, rows)
    return outs


def body(home_rows, guest_rows, home_cluster, guest_cluster, pair_mask):
    slots = home_rows.shape[0] // BLOCK
    y, z, x, h, k = (lax.axis_index(a) for a in AXES)

    def device_of(yy, kk):
        return (((yy * NZ + z) * NX + x) * NH + h) * NK + kk

    table = jnp.concatenate([
        lax.dynamic_slice(guest_cluster.reshape(NY, NZ * NX, NH * NK), (y, 0, h * NK + k), (1, NZ * NX, 1)).reshape(-1),
        lax.dynamic_slice_in_dim(home_cluster, device_of(y, 1 - k) * slots, slots),
        lax.dynamic_slice_in_dim(home_cluster, device_of(1 - y, 1 - k) * slots, slots),
    ])
    near_at = jnp.array([NZ * NX], jnp.int32)
    far_at = jnp.array([NZ * NX + slots], jnp.int32)

    def places(nodes):
        back = jnp.array(nodes, jnp.int32)
        return (z - back[:, 0]) % NZ * NX + (x - back[:, 1]) % NX

    def scaled(blocks):
        return jnp.broadcast_to((inverse_norms(blocks) * EXP2_SCALE)[..., None], (*blocks.shape[:2], LANES))

    def zeros(n):
        return jnp.zeros((n, BLOCK, LANES), jnp.float32)

    held = {(0, 0): guest_rows}
    scales, col_parts, arrived = {}, {}, []

    def note(nodes, cols):
        for i, n in enumerate(nodes):
            col_parts.setdefault(n, []).append(cols[i])

    def send(slot, after):
        sends = [(parent, node(parent[0] + dz, parent[1] + dx), dz, dx) for (dz, dx), parent in slot]
        blocks, _ = lax.optimization_barrier((tuple(held[p] for p, _, _, _ in sends), tuple(after)))
        for block, (_, child, dz, dx) in zip(blocks, sends, strict=True):
            held[child] = shift(block, dz, dx)
        return [child for _, child, _, _ in sends]

    far = to_partner(home_rows).reshape(slots, BLOCK, -1)
    newest = [(0, 0), *send(SLOTS[0], [])]
    near = to_sibling(lax.optimization_barrier((home_rows, held[newest[1]]))[0]).reshape(slots, BLOCK, -1)
    near_scale = scaled(near)
    near_rows, back_rows, all_rows = zeros(slots), zeros(slots), None
    backlog, done = [], []
    for s in range(1, len(SLOTS) + 1):
        if s < len(SLOTS):
            coming = send(SLOTS[s], [held[n] for n in newest] + done)
        done = []
        if s == IDS_AT:
            home_cluster, guest_cluster, _ = lax.optimization_barrier(
                (home_cluster, guest_cluster, tuple(held[n] for n in newest))
            )
        if s < FAR_FROM:
            near_rows, cols, scale = pairs(
                table, places(newest), near_at, [held[n] for n in newest], None, near, near_scale, near_rows
            )
            backlog += newest
        else:
            if s == FAR_FROM:
                far, _ = lax.optimization_barrier((far, tuple(held[n] for n in newest)))
                far_scale = scaled(far)
                blocks = jnp.concatenate([near, far])
                all_scale = jnp.concatenate([near_scale, far_scale])
                all_rows = jnp.concatenate([near_rows, zeros(slots)])
            all_rows, cols, scale = pairs(
                table, places(newest), near_at, [held[n] for n in newest], None, blocks, all_scale, all_rows
            )
            turns = len(SLOTS) - s
            if turns > 0:
                some = backlog[: -(-len(backlog) // turns)]
                backlog = backlog[len(some) :]
                back_rows, back_cols = pairs(
                    table, places(some), far_at, [held[n] for n in some], jnp.stack([scales[n] for n in some]),
                    far, far_scale, back_rows,
                )
                note(some, back_cols)
                done.append(back_cols)
        for i, n in enumerate(newest):
            scales[n] = scale[i]
        note(newest, cols)
        done.append(cols)
        newest = coming
    near_rows, far_rows = all_rows[:slots], all_rows[slots:] + back_rows

    order = [node(dz, dx) for dz in range(NZ) for dx in range(NX)]
    by_node = jnp.stack([functools.reduce(jnp.add, col_parts[n]) for n in order]).reshape(NZ, NX, BLOCK)
    source_z = (z - jnp.arange(NZ)) % NZ
    source_x = (x - jnp.arange(NX)) % NX
    outgoing = by_node[source_z][:, source_x].reshape(NZ * NX, BLOCK)
    incoming = lax.all_to_all(outgoing, ("z", "x"), 0, 0, tiled=True)
    guest_density = jnp.sum(incoming, axis=0)
    home_density = to_sibling(jnp.sum(near_rows, axis=-1)) + to_partner(jnp.sum(far_rows, axis=-1))

    home_ids = lax.dynamic_slice_in_dim(home_cluster, device_of(y, k) * slots, slots)
    guest_id = lax.dynamic_slice_in_dim(guest_cluster, device_of(y, k), 1)

    def members(ids):
        count = jnp.sum((home_cluster[None, :] == ids[:, None]).astype(jnp.int32), axis=1)
        count = count + jnp.sum((guest_cluster[None, :] == ids[:, None]).astype(jnp.int32), axis=1)
        return count.astype(jnp.float32)

    home_score = jnp.log(1.0 + home_density) - jnp.log(members(home_ids))[:, None]
    guest_score = jnp.log(1.0 + guest_density) - jnp.log(members(guest_id))
    return home_score.reshape(-1), guest_score


def solution(mesh):
    whole = Mesh(mesh.devices.reshape(NY, NZ, NX, NH, NK), AXES)
    placed = (P(AXES, None), P(AXES, None), P(), P(), P(AXES, None, None))
    return jax.shard_map(
        body, mesh=whole, in_specs=placed, out_specs=(P(AXES), P(AXES)), check_vma=False
    )
```

```python
import functools
import math

import jax
import jax.numpy as jnp
from jax import lax
from jax.experimental import pallas as pl
from jax.experimental.pallas import tpu as pltpu
from jax.sharding import Mesh
from jax.sharding import PartitionSpec as P

BLOCK = 256
LANES = 128
SHARPNESS = 30.0
EPSILON = 1e-06
EXP2_SCALE = SHARPNESS / math.log(2.0)
UNROLL = 4
FAR_FROM = 4
IDS_AT = 3

NY, NZ, NX, NH, NK = 2, 8, 4, 2, 2
AXES = ("y", "z", "x", "h", "k")

SLOTS = (
    ( ((0, 1), ((0, 0),)), ((-1, 0), ((0, 0),)), ((0, -1), ((0, 0),)), ((1, 0), ((0, 0),)) ),
    ( ((1, 0), ((1, 0),)), ((-1, 0), ((-1, 0),)), ((0, 1), ((0, 1),)), ((0, -1), ((-1, 0),)) ),
    ( ((0, 1), ((2, 0),)), ((0, -1), ((1, 0),)), ((-1, 0), ((-2, 0),)), ((1, 0), ((2, 0),)) ),
    ( ((-1, 0), ((0, 2), (0, 1),)), ((1, 0), ((0, 2), (0, 1),)), ((0, 1), ((3, 0), (-3, 0),)), ((0, -1), ((3, 0), (-3, 0),)) ),
    ( ((-1, 0), ((3, -1), (-3, -1),)), ((0, 1), ((3, 1), (-3, 1),)), ((0, -1), ((-2, 0),)), ((1, 0), ((3, 1), (-3, 1),)) ),
    ( ((0, 1), ((-2, 1),)), ((0, -1), ((2, -1),)), ((1, 0), ((3, 0),)), ((-1, 0), ((-3, 2),)) ),
)


def node(dz, dx):
    return ((dz + 3) % NZ - 3, (dx + 1) % NX - 1)


def shift(value, dz, dx):
    if dx == 0:
        return lax.ppermute(value, "z", [(i, (i + dz) % NZ) for i in range(NZ)])
    if dz == 0:
        return lax.ppermute(value, "x", [(i, (i + dx) % NX) for i in range(NX)])
    return lax.ppermute(
        value,
        ("z", "x"),
        [(z * NX + x, (z + dz) % NZ * NX + (x + dx) % NX) for z in range(NZ) for x in range(NX)],
    )


def to_sibling(value):
    return lax.ppermute(value, "k", [(0, 1), (1, 0)])


def to_partner(value):
    return lax.ppermute(value, ("y", "k"), [(0, 3), (1, 2), (2, 1), (3, 0)])


def inverse_norms(rows):
    values = rows.astype(jnp.float32)
    return 1.0 / jnp.sqrt(jnp.sum(values * values, axis=-1) + EPSILON)


def lane_sums(values):
    high = values.astype(jnp.bfloat16)
    rest = values - high.astype(jnp.float32)
    middle = rest.astype(jnp.bfloat16)
    low = (rest - middle.astype(jnp.float32)).astype(jnp.bfloat16)
    terms = jnp.concatenate([high, middle, low], axis=1)
    ones = jnp.ones((8, terms.shape[1]), jnp.bfloat16)
    return lax.dot_general(ones, terms, (((1,), (1,)), ((), ())), preferred_element_type=jnp.float32)[:1]


def pair_kernel(news, olds, sizes, first_far, table, *refs):
    arrays, refs = refs[: len(sizes)], refs[len(sizes) :]
    blocks, scale, rows_in, cols_in, norms_in, turn, rows, cols_out, norms, next_turn, held, cols, listed, places, sems = refs
    n_new, n_old, n_set = len(news), len(olds), blocks.shape[0]
    z, x = table[table.shape[0] - 2], table[table.shape[0] - 1]
    copies, first = [], 0
    for a, (array, size) in enumerate(zip(arrays, sizes, strict=True)):
        copies.append((first, pltpu.make_async_copy(array, held.at[pl.ds(first, size)], sems.at[a])))
        first += size
    for _, copy in copies:
        copy.start()
    for g, (dz, dx) in enumerate([*news, *olds]):
        places[g] = lax.rem(z - dz + NZ, NZ) * NX + lax.rem(x - dx + NX, NX)

    def list_pairs(first_guest, last_guest, first_block):
        def list_guest(g, count):
            wanted = table[places[g]]

            def list_pair(r, count):
                listed[0, count] = r
                listed[1, count] = g
                return count + jnp.where(table[NZ * NX + r] == wanted, 1, 0)

            return lax.fori_loop(first_block, n_set, list_pair, count)

        count = lax.fori_loop(first_guest, last_guest, list_guest, 0)
        for u in range(UNROLL):
            listed[0, count + u] = first_block
            listed[1, count + u] = first_guest
        return count

    def run_pairs(count):
        @pl.loop(0, lax.div(count + UNROLL - 1, UNROLL))
        def _(step):
            for u in range(UNROLL):
                at = step * UNROLL + u
                r, g = listed[0, at], listed[1, at]
                keep = jnp.where(at < count, 1.0, 0.0)
                products = lax.dot_general(
                    blocks[r], held[g], (((1,), (1,)), ((), ())), preferred_element_type=jnp.float32
                )
                norm = norms[pl.ds(places[g], 1), :]
                total = rows[r]
                for half in range(BLOCK // LANES):
                    lanes = slice(half * LANES, (half + 1) * LANES)
                    tile = jnp.exp2(products[:, lanes] * scale[r] * norm[:, lanes]) * keep
                    total = total + tile
                    cols[g, :, lanes] += jnp.sum(tile.reshape(BLOCK // 8, 8, LANES), axis=0)
                rows[r] = total

    count = list_pairs(0, n_new, 0)
    cols[...] = jnp.zeros_like(cols)
    rows[...] = rows_in[...]
    cols_out[...] = cols_in[...]
    norms[...] = norms_in[...]
    next_turn[...] = turn[...]
    for first, copy in copies:
        if first < n_new:
            copy.wait()

    @pl.loop(0, n_new)
    def _(g):
        squares = jnp.zeros((BLOCK, LANES), jnp.float32)
        for part in range(held.shape[2] // LANES):
            values = held[g, :, part * LANES : (part + 1) * LANES].astype(jnp.float32)
            squares = squares + values * values
        norms[pl.ds(places[g], 1), :] = 1.0 / jnp.sqrt(lane_sums(squares) + EPSILON)

    run_pairs(count)
    if n_old:
        count = list_pairs(n_new, n_new + n_old, first_far)
        for first, copy in copies:
            if first >= n_new:
                copy.wait()
        run_pairs(count)

    @pl.loop(0, n_new + n_old)
    def _(g):
        cols_out[pl.ds(places[g], 1), :] += jnp.sum(cols[g], axis=0, keepdims=True)


def pairs(table, news, olds, arrays, first_far, blocks, scale, rows, cols, norms, turn):
    n_guest, n_set = len(news) + len(olds), blocks.shape[0]
    sizes = [a.shape[0] for a in arrays]
    smem = pl.BlockSpec(memory_space=pltpu.SMEM)
    vmem = pl.BlockSpec(memory_space=pltpu.VMEM)
    tiles = (len(news) * n_set + len(olds) * (n_set - first_far)) // 3
    return pl.pallas_call(
        functools.partial(pair_kernel, news, olds, sizes, first_far),
        in_specs=[smem] + [pl.BlockSpec(memory_space=pltpu.HBM)] * len(arrays) + [vmem] * 6,
        out_specs=[vmem] * 4,
        out_shape=[jax.ShapeDtypeStruct(v.shape, jnp.float32) for v in (rows, cols, norms, turn)],
        scratch_shapes=[
            pltpu.VMEM((n_guest, *arrays[0].shape[1:]), jnp.bfloat16),
            pltpu.VMEM((n_guest, 8, BLOCK), jnp.float32),
            pltpu.SMEM((2, n_guest * n_set + UNROLL), jnp.int32),
            pltpu.SMEM((n_guest,), jnp.int32),
            pltpu.SemaphoreType.DMA((len(arrays),)),
        ],
        input_output_aliases={1 + len(arrays) + 2 + j: j for j in range(3)},
        compiler_params=pltpu.CompilerParams(vmem_limit_bytes=63 << 20),
        cost_estimate=pl.CostEstimate(
            flops=tiles * 4 * BLOCK * BLOCK * 768, bytes_accessed=tiles * 400000, transcendentals=tiles * BLOCK * BLOCK
        ),
        name="pairs",
    )(table, *arrays, blocks, scale, rows, cols, norms, turn)


def body(home_rows, guest_rows, home_cluster, guest_cluster, pair_mask):
    slots = home_rows.shape[0] // BLOCK
    y, z, x, h, k = (lax.axis_index(a) for a in AXES)

    def device_of(yy, kk):
        return (((yy * NZ + z) * NX + x) * NH + h) * NK + kk

    table = jnp.concatenate([
        lax.dynamic_slice(guest_cluster.reshape(NY, NZ * NX, NH * NK), (y, 0, h * NK + k), (1, NZ * NX, 1)).reshape(-1),
        lax.dynamic_slice_in_dim(home_cluster, device_of(y, 1 - k) * slots, slots),
        lax.dynamic_slice_in_dim(home_cluster, device_of(1 - y, 1 - k) * slots, slots),
        jnp.stack([z, x]),
    ])

    def scaled(blocks):
        return jnp.broadcast_to((inverse_norms(blocks) * EXP2_SCALE)[..., None], (*blocks.shape[:2], LANES))

    def zeros(n):
        return jnp.zeros((n, BLOCK, LANES), jnp.float32)

    stacks = {((0, 0),): guest_rows[None]}

    def one(n):
        for nodes, blocks in stacks.items():
            if n in nodes:
                return blocks[nodes.index(n)]
        raise ValueError(n)

    def send(slot, after):
        sends = [(stacks[p] if p in stacks else jnp.stack([one(n) for n in p]), p, d) for d, p in slot]
        blocks, _ = lax.optimization_barrier((tuple(b for b, _, _ in sends), tuple(after)))
        made = []
        for block, (_, parents, (dz, dx)) in zip(blocks, sends, strict=True):
            made.append(tuple(node(n[0] + dz, n[1] + dx) for n in parents))
            stacks[made[-1]] = shift(block, dz, dx)
        return made

    def flat(groups):
        return [n for nodes in groups for n in nodes]

    far = to_partner(home_rows).reshape(slots, BLOCK, -1)
    near = to_sibling(home_rows).reshape(slots, BLOCK, -1)
    newest = [((0, 0),), *send(SLOTS[0][:3], []), *send(SLOTS[0][3:], [near])]
    blocks, scale, rows = near, scaled(near), zeros(slots)
    cols = norms = jnp.zeros((NZ * NX, BLOCK), jnp.float32)
    turn = jnp.zeros((8, LANES), jnp.float32)
    backlog, done = [], []
    for s in range(1, len(SLOTS) + 1):
        came = tuple(stacks[p] for p in newest)
        coming = send(SLOTS[s], [*came, *done]) if s < len(SLOTS) else []
        if s == IDS_AT:
            home_cluster, guest_cluster, _ = lax.optimization_barrier((home_cluster, guest_cluster, came))
        olds = []
        if s == FAR_FROM:
            far, _ = lax.optimization_barrier((far, came))
            blocks = jnp.concatenate([near, far])
            scale = jnp.concatenate([scale, scaled(far)])
            rows = jnp.concatenate([rows, zeros(slots)])
            olds = backlog
        rows, cols, norms, turn = pairs(
            table, flat(newest), flat(olds), [stacks[p] for p in [*newest, *olds]], slots, blocks, scale, rows, cols, norms,
            turn,
        )
        backlog = backlog + newest
        done = [turn]
        newest = coming
    near_rows, far_rows = rows[:slots], rows[slots:]

    incoming = lax.all_to_all(cols, ("z", "x"), 0, 0, tiled=True)
    guest_density = jnp.sum(incoming, axis=0)
    home_density = to_sibling(jnp.sum(near_rows, axis=-1)) + to_partner(jnp.sum(far_rows, axis=-1))

    home_ids = lax.dynamic_slice_in_dim(home_cluster, device_of(y, k) * slots, slots)
    guest_id = lax.dynamic_slice_in_dim(guest_cluster, device_of(y, k), 1)

    def members(ids):
        count = jnp.sum((home_cluster[None, :] == ids[:, None]).astype(jnp.int32), axis=1)
        count = count + jnp.sum((guest_cluster[None, :] == ids[:, None]).astype(jnp.int32), axis=1)
        return count.astype(jnp.float32)

    home_score = jnp.log(1.0 + home_density) - jnp.log(members(home_ids))[:, None]
    guest_score = jnp.log(1.0 + guest_density) - jnp.log(members(guest_id))
    return home_score.reshape(-1), guest_score


def solution(mesh):
    whole = Mesh(mesh.devices.reshape(NY, NZ, NX, NH, NK), AXES)
    placed = (P(AXES, None), P(AXES, None), P(), P(), P(AXES, None, None))
    return jax.shard_map(
        body, mesh=whole, in_specs=placed, out_specs=(P(AXES), P(AXES)), check_vma=False
    )
```

```python
import functools
import math

import jax
import jax.numpy as jnp
from jax import lax
from jax.experimental import pallas as pl
from jax.experimental.pallas import tpu as pltpu
from jax.sharding import Mesh
from jax.sharding import PartitionSpec as P

BLOCK = 256
LANES = 128
SHARPNESS = 30.0
EPSILON = 1e-06
EXP2_SCALE = SHARPNESS / math.log(2.0)
UNROLL = 4
VMEM_MIB = 63
FAR_FROM = 4
IDS_AT = 3

NY, NZ, NX, NH, NK = 2, 8, 4, 2, 2
AXES = ("y", "z", "x", "h", "k")

SLOTS = (
    ( ((0, 1), ((0, 0),)), ((-1, 0), ((0, 0),)), ((0, -1), ((0, 0),)), ((1, 0), ((0, 0),)) ),
    ( ((1, 0), ((1, 0),)), ((-1, 0), ((-1, 0),)), ((0, 1), ((0, 1),)), ((0, -1), ((-1, 0),)) ),
    ( ((0, 1), ((2, 0),)), ((0, -1), ((1, 0),)), ((-1, 0), ((-2, 0),)), ((1, 0), ((2, 0),)) ),
    ( ((-1, 0), ((0, 2), (0, 1),)), ((1, 0), ((0, 2), (0, 1),)), ((0, 1), ((3, 0), (-3, 0),)), ((0, -1), ((3, 0), (-3, 0),)) ),
    ( ((-1, 0), ((3, -1), (-3, -1),)), ((0, 1), ((3, 1), (-3, 1),)), ((0, -1), ((-2, 0),)), ((1, 0), ((3, 1), (-3, 1),)) ),
    ( ((0, 1), ((-2, 1),)), ((0, -1), ((2, -1),)), ((1, 0), ((3, 0),)), ((-1, 0), ((-3, 2),)) ),
)


def node(dz, dx):
    return ((dz + 3) % NZ - 3, (dx + 1) % NX - 1)


def shift(value, dz, dx):
    if dx == 0:
        return lax.ppermute(value, "z", [(i, (i + dz) % NZ) for i in range(NZ)])
    if dz == 0:
        return lax.ppermute(value, "x", [(i, (i + dx) % NX) for i in range(NX)])
    return lax.ppermute(
        value,
        ("z", "x"),
        [(z * NX + x, (z + dz) % NZ * NX + (x + dx) % NX) for z in range(NZ) for x in range(NX)],
    )


def to_sibling(value):
    return lax.ppermute(value, "k", [(0, 1), (1, 0)])


def to_partner(value):
    return lax.ppermute(value, ("y", "k"), [(0, 3), (1, 2), (2, 1), (3, 0)])


def three_terms(values):
    high = values.astype(jnp.bfloat16)
    rest = values - high.astype(jnp.float32)
    middle = rest.astype(jnp.bfloat16)
    return high, middle, (rest - middle.astype(jnp.float32)).astype(jnp.bfloat16)


def lane_sums(values):
    terms = jnp.concatenate(three_terms(values), axis=1)
    ones = jnp.ones((8, terms.shape[1]), jnp.bfloat16)
    return lax.dot_general(ones, terms, (((1,), (1,)), ((), ())), preferred_element_type=jnp.float32)[:1]


def as_column(row):
    at = lax.broadcasted_iota(jnp.int32, (16, row.shape[1]), 0)
    terms = jnp.zeros((16, row.shape[1]), jnp.float32)
    for i, term in enumerate(three_terms(row)):
        terms = jnp.where(at == i, term.astype(jnp.float32), terms)
    ones = jnp.ones((16, LANES), jnp.bfloat16)
    return lax.dot_general(
        terms.astype(jnp.bfloat16), ones, (((0,), (0,)), ((), ())), preferred_element_type=jnp.float32
    )


def pair_kernel(news, olds, sizes, n_sets, first, table, *refs):
    arrays, refs = refs[: len(sizes)], refs[len(sizes) :]
    sets, refs = refs[:n_sets], refs[n_sets:]
    before, refs = ((), refs) if first else (refs[:5], refs[5:])
    rows, cols, norms, scale, next_turn, held, blocks, columns, sums, listed, places, sems = refs
    n_new, n_guest = len(news), len(news) + len(olds)
    n_set, n_each = blocks.shape[0], sets[0].shape[0]
    z, x = table[table.shape[0] - 2], table[table.shape[0] - 1]

    guest_copies, at = [], 0
    for a, (array, size) in enumerate(zip(arrays, sizes, strict=True)):
        guest_copies.append((at, pltpu.make_async_copy(array, held.at[pl.ds(at, size)], sems.at[a])))
        at += size
    set_copies = [
        pltpu.make_async_copy(one, blocks.at[pl.ds(j * n_each, n_each)], sems.at[len(sizes) + j])
        for j, one in enumerate(sets)
    ]
    for at, copy in guest_copies:
        if at < n_new:
            copy.start()
    for copy in set_copies:
        copy.start()
    for at, copy in guest_copies:
        if at >= n_new:
            copy.start()
    for g, (dz, dx) in enumerate([*news, *olds]):
        places[g] = lax.rem(z - dz + NZ, NZ) * NX + lax.rem(x - dx + NX, NX)

    def list_pairs(first_guest, last_guest, first_block):
        def list_guest(g, count):
            wanted = table[places[g]]

            def list_pair(r, count):
                listed[0, count] = r
                listed[1, count] = g
                return count + jnp.where(table[NZ * NX + r] == wanted, 1, 0)

            return lax.fori_loop(first_block, n_set, list_pair, count)

        count = lax.fori_loop(first_guest, last_guest, list_guest, 0)
        for u in range(UNROLL):
            listed[0, count + u] = first_block
            listed[1, count + u] = first_guest
        return count

    def run_pairs(count):
        @pl.loop(0, lax.div(count + UNROLL - 1, UNROLL))
        def _(step):
            for u in range(UNROLL):
                at = step * UNROLL + u
                r, g = listed[0, at], listed[1, at]
                keep = jnp.where(at < count, 1.0, 0.0)
                products = lax.dot_general(
                    held[g], blocks[r], (((1,), (1,)), ((), ())), preferred_element_type=jnp.float32
                )
                across, down = scale[pl.ds(r, 1), :], columns[g]
                total = sums[g]
                for half in range(BLOCK // LANES):
                    lanes = slice(half * LANES, (half + 1) * LANES)
                    tile = jnp.exp2(products[:, lanes] * down * across[:, lanes]) * keep
                    total = total + tile
                    rows[r, :, lanes] += jnp.sum(tile.reshape(BLOCK // 8, 8, LANES), axis=0)
                sums[g] = total

    count = list_pairs(0, n_new, 0)
    if first:
        for out in (rows, cols, norms, scale, next_turn):
            out[...] = jnp.zeros_like(out)
    else:
        for out, value in zip((rows, cols, norms, scale, next_turn), before, strict=True):
            out[...] = value[...]
    sums[...] = jnp.zeros_like(sums)
    for at, copy in guest_copies:
        if at < n_new:
            copy.wait()

    def inverse_norms(block):
        squares = jnp.zeros((BLOCK, LANES), jnp.float32)
        for part in range(block.shape[1] // LANES):
            values = block[:, part * LANES : (part + 1) * LANES].astype(jnp.float32)
            squares = squares + values * values
        return 1.0 / jnp.sqrt(lane_sums(squares) + EPSILON)

    @pl.loop(0, n_new)
    def _(g):
        norms[pl.ds(places[g], 1), :] = inverse_norms(held.at[g])

    @pl.loop(0, n_guest)
    def _(g):
        columns[g] = as_column(norms[pl.ds(places[g], 1), :])

    for copy in set_copies:
        copy.wait()
    if first or olds:

        @pl.loop(n_set - n_each, n_set)
        def _(r):
            scale[pl.ds(r, 1), :] = inverse_norms(blocks.at[r]) * EXP2_SCALE

    run_pairs(count)
    if olds:
        count = list_pairs(n_new, n_guest, n_set - n_each)
        for at, copy in guest_copies:
            if at >= n_new:
                copy.wait()
        run_pairs(count)

    @pl.loop(0, n_guest)
    def _(g):
        cols[pl.ds(places[g], 1), :] += lane_sums(sums[g])


def pairs(table, news, olds, arrays, sets, running):
    n_guest, n_set = len(news) + len(olds), sum(one.shape[0] for one in sets)
    smem, vmem, hbm = (pl.BlockSpec(memory_space=m) for m in (pltpu.SMEM, pltpu.VMEM, pltpu.HBM))
    first = running is None
    tiles = (len(news) * n_set + len(olds) * sets[-1].shape[0]) // 3
    shapes = [(2 * sets[0].shape[0], 8, BLOCK), (NZ * NX, BLOCK), (NZ * NX, BLOCK), (16, BLOCK), (8, LANES)]
    return pl.pallas_call(
        functools.partial(pair_kernel, news, olds, [a.shape[0] for a in arrays], len(sets), first),
        in_specs=[smem] + [hbm] * (len(arrays) + len(sets)) + [vmem] * (0 if first else 5),
        out_specs=[vmem] * 5,
        out_shape=[jax.ShapeDtypeStruct(shape, jnp.float32) for shape in shapes],
        scratch_shapes=[
            pltpu.VMEM((n_guest, *arrays[0].shape[1:]), jnp.bfloat16),
            pltpu.VMEM((n_set, *arrays[0].shape[1:]), jnp.bfloat16),
            pltpu.VMEM((n_guest, BLOCK, LANES), jnp.float32),
            pltpu.VMEM((n_guest, BLOCK, LANES), jnp.float32),
            pltpu.SMEM((2, n_guest * n_set + UNROLL), jnp.int32),
            pltpu.SMEM((n_guest,), jnp.int32),
            pltpu.SemaphoreType.DMA((len(arrays) + len(sets),)),
        ],
        compiler_params=pltpu.CompilerParams(vmem_limit_bytes=VMEM_MIB << 20),
        cost_estimate=pl.CostEstimate(
            flops=tiles * 4 * BLOCK * BLOCK * 768, bytes_accessed=tiles * 400000, transcendentals=tiles * BLOCK * BLOCK
        ),
        name="pairs",
    )(table, *arrays, *sets, *([] if first else running))


def body(home_rows, guest_rows, home_cluster, guest_cluster, pair_mask):
    slots = home_rows.shape[0] // BLOCK
    y, z, x, h, k = (lax.axis_index(a) for a in AXES)

    def device_of(yy, kk):
        return (((yy * NZ + z) * NX + x) * NH + h) * NK + kk

    table = jnp.concatenate([
        lax.dynamic_slice(guest_cluster.reshape(NY, NZ * NX, NH * NK), (y, 0, h * NK + k), (1, NZ * NX, 1)).reshape(-1),
        lax.dynamic_slice_in_dim(home_cluster, device_of(y, 1 - k) * slots, slots),
        lax.dynamic_slice_in_dim(home_cluster, device_of(1 - y, 1 - k) * slots, slots),
        jnp.stack([z, x]),
    ])

    stacks = {((0, 0),): guest_rows[None]}

    def one(n):
        for nodes, blocks in stacks.items():
            if n in nodes:
                return blocks[nodes.index(n)]
        raise ValueError(n)

    def send(slot, after):
        sends = [(stacks[p] if p in stacks else jnp.stack([one(n) for n in p]), p, d) for d, p in slot]
        blocks, _ = lax.optimization_barrier((tuple(b for b, _, _ in sends), tuple(after)))
        made = []
        for block, (_, parents, (dz, dx)) in zip(blocks, sends, strict=True):
            made.append(tuple(node(n[0] + dz, n[1] + dx) for n in parents))
            stacks[made[-1]] = shift(block, dz, dx)
        return made

    def flat(groups):
        return [n for nodes in groups for n in nodes]

    far = to_partner(home_rows).reshape(slots, BLOCK, -1)
    near = to_sibling(home_rows).reshape(slots, BLOCK, -1)
    newest = [((0, 0),), *send(SLOTS[0][:3], []), *send(SLOTS[0][3:], [near])]
    sets, running = [near], None
    backlog, done = [], []
    for s in range(1, len(SLOTS) + 1):
        came = tuple(stacks[p] for p in newest)
        coming = send(SLOTS[s], [*came, *done]) if s < len(SLOTS) else []
        if s == IDS_AT:
            home_cluster, guest_cluster, _ = lax.optimization_barrier((home_cluster, guest_cluster, came))
        olds = []
        if s == FAR_FROM:
            far, _ = lax.optimization_barrier((far, came))
            sets = [near, far]
            olds = backlog
        running = pairs(table, flat(newest), flat(olds), [stacks[p] for p in [*newest, *olds]], sets, running)
        backlog = backlog + newest
        done = [running[4]]
        newest = coming
    rows, cols = jnp.sum(running[0], axis=1), running[1]

    incoming = lax.all_to_all(cols, ("z", "x"), 0, 0, tiled=True)
    guest_density = jnp.sum(incoming, axis=0)
    home_density = to_sibling(rows[:slots]) + to_partner(rows[slots:])

    home_ids = lax.dynamic_slice_in_dim(home_cluster, device_of(y, k) * slots, slots)
    guest_id = lax.dynamic_slice_in_dim(guest_cluster, device_of(y, k), 1)

    def members(ids):
        count = jnp.sum((home_cluster[None, :] == ids[:, None]).astype(jnp.int32), axis=1)
        count = count + jnp.sum((guest_cluster[None, :] == ids[:, None]).astype(jnp.int32), axis=1)
        return count.astype(jnp.float32)

    home_score = jnp.log(1.0 + home_density) - jnp.log(members(home_ids))[:, None]
    guest_score = jnp.log(1.0 + guest_density) - jnp.log(members(guest_id))
    return home_score.reshape(-1), guest_score


def solution(mesh):
    whole = Mesh(mesh.devices.reshape(NY, NZ, NX, NH, NK), AXES)
    placed = (P(AXES, None), P(AXES, None), P(), P(), P(AXES, None, None))
    return jax.shard_map(
        body, mesh=whole, in_specs=placed, out_specs=(P(AXES), P(AXES)), check_vma=False
    )
```

```python
import functools
import math

import jax
import jax.numpy as jnp
from jax import lax
from jax.experimental import pallas as pl
from jax.experimental.pallas import tpu as pltpu
from jax.sharding import Mesh
from jax.sharding import PartitionSpec as P

BLOCK = 256
LANES = 128
SHARPNESS = 30.0
EPSILON = 1e-06
EXP2_SCALE = SHARPNESS / math.log(2.0)
UNROLL = 6
GROUP = 4
AHEAD = 6
VMEM_MIB = 63
FAR_FROM = 4
IDS_AT = 3

NY, NZ, NX, NH, NK = 2, 8, 4, 2, 2
AXES = ("y", "z", "x", "h", "k")

SLOTS = (
    ( ((0, -1), ((0, 0),)), ((-1, 0), ((0, 0),)), ((1, 0), ((0, 0),)), ((0, 1), ((0, 0),)) ),
    ( ((-1, 0), ((-1, 0),)), ((1, 0), ((1, 0),)), ((0, -1), ((-1, 0),)), ((0, 1), ((0, 1),)) ),
    ( ((1, 0), ((0, 2),)), ((0, 1), ((2, 0),)), ((0, -1), ((2, 0),)), ((-1, 0), ((-2, 0),)) ),
    ( ((-1, 0), ((2, 1), (2, -1),)), ((0, -1), ((-3, 0), (-2, 0),)), ((1, 0), ((2, 1), (2, -1),)), ((0, 1), ((-3, 0), (-2, 0),)) ),
    ( ((1, 0), ((3, 1), (3, -1),)), ((0, 1), ((3, 1), (3, -1),)), ((-1, 0), ((0, 1), (-3, 0),)), ((0, -1), ((-3, -1), (-2, -1),)) ),
    ( ((-1, 0), ((0, 2),)), ((0, -1), ((2, -1),)), ((1, 0), ((3, 2),)) ),
)


def node(dz, dx):
    return ((dz + 3) % NZ - 3, (dx + 1) % NX - 1)


def shift(value, dz, dx):
    if dx == 0:
        return lax.ppermute(value, "z", [(i, (i + dz) % NZ) for i in range(NZ)])
    if dz == 0:
        return lax.ppermute(value, "x", [(i, (i + dx) % NX) for i in range(NX)])
    return lax.ppermute(
        value,
        ("z", "x"),
        [(z * NX + x, (z + dz) % NZ * NX + (x + dx) % NX) for z in range(NZ) for x in range(NX)],
    )


def to_sibling(value):
    return lax.ppermute(value, "k", [(0, 1), (1, 0)])


def to_partner(value):
    return lax.ppermute(value, ("y", "k"), [(0, 3), (1, 2), (2, 1), (3, 0)])


def three_terms(values):
    high = values.astype(jnp.bfloat16)
    rest = values - high.astype(jnp.float32)
    middle = rest.astype(jnp.bfloat16)
    return high, middle, (rest - middle.astype(jnp.float32)).astype(jnp.bfloat16)


def lane_sums(values):
    terms = jnp.concatenate(three_terms(values), axis=1)
    ones = jnp.ones((8, terms.shape[1]), jnp.bfloat16)
    return lax.dot_general(ones, terms, (((1,), (1,)), ((), ())), preferred_element_type=jnp.float32)[:1]


def lane_totals(values):
    terms = jnp.concatenate(three_terms(values), axis=1)
    ones = jnp.ones((terms.shape[1], LANES), jnp.bfloat16)
    return lax.dot_general(terms, ones, (((1,), (0,)), ((), ())), preferred_element_type=jnp.float32)


def squares(block):
    total = None
    for part in range(block.shape[1] // LANES):
        values = block[:, part * LANES : (part + 1) * LANES].astype(jnp.float32)
        total = values * values if total is None else total + values * values
    return total


def pair_kernel(news, olds, sizes, n_sets, first, table, *refs):
    arrays, refs = refs[: len(sizes)], refs[len(sizes) :]
    sets, refs = refs[:n_sets], refs[n_sets:]
    before, refs = ((), refs) if first else (refs[:4], refs[4:])
    rows, cols, scale, next_turn, held, blocks, columns, sums, added, listed, places, sems, set_sems = refs
    n_new, n_guest = len(news), len(news) + len(olds)
    n_set, n_each = blocks.shape[0], sets[0].shape[0]
    z, x = table[table.shape[0] - 2], table[table.shape[0] - 1]

    guest_copies, at = [], 0
    for a, (array, size) in enumerate(zip(arrays, sizes, strict=True)):
        guest_copies.append((at, pltpu.make_async_copy(array, held.at[pl.ds(at, size)], sems.at[a])))
        at += size
    def start_block(r):
        for j in range(n_sets):

            @pl.when((r >= j * n_each) & (r < (j + 1) * n_each))
            def _(j=j):
                pltpu.make_async_copy(sets[j].at[r - j * n_each], blocks.at[r], set_sems.at[r]).start()

    for at, copy in guest_copies:
        if at < n_new:
            copy.start()
    for g, (dz, dx) in enumerate([*news, *olds]):
        places[g] = lax.rem(z - dz + NZ, NZ) * NX + lax.rem(x - dx + NX, NX)

    def list_pairs(first_guest, last_guest, first_block):
        def list_block(r, count):
            own = table[NZ * NX + r]
            for g in range(first_guest, last_guest):
                listed[0, count] = r
                listed[1, count] = g
                count = count + jnp.where(table[places[g]] == own, 1, 0)
            return count

        count = lax.fori_loop(first_block, n_set, list_block, 0)
        for u in range(UNROLL):
            listed[0, count + u] = first_block
            listed[1, count + u] = first_guest
        return count

    def wait_blocks(start, stop):
        def wait_block(r, _):
            pltpu.make_async_copy(sets[0].at[0], blocks.at[r], set_sems.at[r]).wait()
            start_block(r + AHEAD)
            return 0

        lax.fori_loop(start, stop, wait_block, 0)
        return jnp.maximum(start, stop)

    def run_pairs(count, waited):
        def run_step(step, waited):
            last = jnp.minimum(step * UNROLL + UNROLL, count) - 1
            waited = wait_blocks(waited, listed[0, last] + 1)
            for u in range(UNROLL):
                at = step * UNROLL + u
                r, g = listed[0, at], listed[1, at]
                keep = jnp.where(at < count, 1.0, 0.0)
                products = lax.dot_general(
                    held[g], blocks[r], (((1,), (1,)), ((), ())), preferred_element_type=jnp.float32
                )
                across, down = scale[pl.ds(r, 1), :], columns[g]
                total = sums[g]
                for half in range(BLOCK // LANES):
                    lanes = slice(half * LANES, (half + 1) * LANES)
                    tile = jnp.exp2(products[:, lanes] * down * across[:, lanes]) * keep
                    total = total + tile
                    rows[r, :, lanes] += jnp.sum(tile.reshape(BLOCK // 8, 8, LANES), axis=0)
                sums[g] = total
            return waited

        return lax.fori_loop(0, lax.div(count + UNROLL - 1, UNROLL), run_step, waited)

    def in_groups(start, stop, task):
        size = min(GROUP, stop - start)

        @pl.loop(0, -(-(stop - start) // size))
        def _(step):
            for u in range(size):
                task(jnp.minimum(start + step * size + u, stop - 1))

    def set_column(g):
        columns[g] = 1.0 / jnp.sqrt(lane_totals(squares(held.at[g])) + EPSILON)

    def set_scale(r):
        scale[pl.ds(r, 1), :] = EXP2_SCALE / jnp.sqrt(lane_sums(squares(blocks.at[r])) + EPSILON)

    def set_col_sums(g):
        cols[places[g]] = added[places[g]] + lane_sums(sums[g])

    count = list_pairs(0, n_new, 0)
    if first:
        for out in (rows, cols, scale, next_turn):
            out[...] = jnp.zeros_like(out)
    else:
        for out, value in zip((rows, cols, scale, next_turn), before, strict=True):
            out[...] = value[...]
    sums[...] = jnp.zeros_like(sums)
    for at, copy in guest_copies:
        if at < n_new:
            copy.wait()
    for r in range(AHEAD):
        start_block(r)
    for at, copy in guest_copies:
        if at >= n_new:
            copy.start()
    in_groups(0, n_new, set_column)
    waited = 0
    if first or olds:
        waited = wait_blocks(0, n_set)
        in_groups(n_set - n_each, n_set, set_scale)
    waited = run_pairs(count, waited)
    if olds:
        count = list_pairs(n_new, n_guest, n_set - n_each)
        for at, copy in guest_copies:
            if at >= n_new:
                copy.wait()
        in_groups(n_new, n_guest, set_column)
        waited = run_pairs(count, waited)
    wait_blocks(waited, n_set)
    added[...] = cols[...]
    in_groups(0, n_guest, set_col_sums)


def pairs(table, news, olds, arrays, sets, running):
    n_guest, n_set = len(news) + len(olds), sum(one.shape[0] for one in sets)
    smem, vmem, hbm = (pl.BlockSpec(memory_space=m) for m in (pltpu.SMEM, pltpu.VMEM, pltpu.HBM))
    first = running is None
    tiles = (len(news) * n_set + len(olds) * sets[-1].shape[0]) // 3
    shapes = [(2 * sets[0].shape[0], 8, BLOCK), (NZ * NX, 1, BLOCK), (16, BLOCK), (8, LANES)]
    return pl.pallas_call(
        functools.partial(pair_kernel, news, olds, [a.shape[0] for a in arrays], len(sets), first),
        in_specs=[smem] + [hbm] * (len(arrays) + len(sets)) + [vmem] * (0 if first else 4),
        out_specs=[vmem] * 4,
        out_shape=[jax.ShapeDtypeStruct(shape, jnp.float32) for shape in shapes],
        scratch_shapes=[
            pltpu.VMEM((n_guest, *arrays[0].shape[1:]), jnp.bfloat16),
            pltpu.VMEM((n_set, *arrays[0].shape[1:]), jnp.bfloat16),
            pltpu.VMEM((n_guest, BLOCK, LANES), jnp.float32),
            pltpu.VMEM((n_guest, BLOCK, LANES), jnp.float32),
            pltpu.VMEM(shapes[1], jnp.float32),
            pltpu.SMEM((2, n_guest * n_set + UNROLL), jnp.int32),
            pltpu.SMEM((n_guest,), jnp.int32),
            pltpu.SemaphoreType.DMA((len(arrays),)),
            pltpu.SemaphoreType.DMA((n_set,)),
        ],
        compiler_params=pltpu.CompilerParams(vmem_limit_bytes=VMEM_MIB << 20),
        cost_estimate=pl.CostEstimate(
            flops=tiles * 4 * BLOCK * BLOCK * 768, bytes_accessed=tiles * 400000, transcendentals=tiles * BLOCK * BLOCK
        ),
        name="pairs",
    )(table, *arrays, *sets, *([] if first else running))


def body(home_rows, guest_rows, home_cluster, guest_cluster, pair_mask):
    slots = home_rows.shape[0] // BLOCK
    y, z, x, h, k = (lax.axis_index(a) for a in AXES)

    def device_of(yy, kk):
        return (((yy * NZ + z) * NX + x) * NH + h) * NK + kk

    table = jnp.concatenate([
        lax.dynamic_slice(guest_cluster.reshape(NY, NZ * NX, NH * NK), (y, 0, h * NK + k), (1, NZ * NX, 1)).reshape(-1),
        lax.dynamic_slice_in_dim(home_cluster, device_of(y, 1 - k) * slots, slots),
        lax.dynamic_slice_in_dim(home_cluster, device_of(1 - y, 1 - k) * slots, slots),
        jnp.stack([z, x]),
    ])

    stacks = {((0, 0),): guest_rows[None]}

    def one(n):
        for nodes, blocks in stacks.items():
            if n in nodes:
                return blocks[nodes.index(n)]
        raise ValueError(n)

    def send(slot, after):
        sends = [(stacks[p] if p in stacks else jnp.stack([one(n) for n in p]), p, d) for d, p in slot]
        blocks, _ = lax.optimization_barrier((tuple(b for b, _, _ in sends), tuple(after)))
        made = []
        for block, (_, parents, (dz, dx)) in zip(blocks, sends, strict=True):
            made.append(tuple(node(n[0] + dz, n[1] + dx) for n in parents))
            stacks[made[-1]] = shift(block, dz, dx)
        return made

    def flat(groups):
        return [n for nodes in groups for n in nodes]

    far = to_partner(home_rows).reshape(slots, BLOCK, -1)
    near = to_sibling(home_rows).reshape(slots, BLOCK, -1)
    newest = [((0, 0),), *send(SLOTS[0][:3], []), *send(SLOTS[0][3:], [near])]
    sets, running = [near], None
    backlog, done = [], []
    for s in range(1, len(SLOTS) + 1):
        came = tuple(stacks[p] for p in newest)
        coming = send(SLOTS[s], [*came, *done]) if s < len(SLOTS) else []
        if s == IDS_AT:
            home_cluster, guest_cluster, _ = lax.optimization_barrier((home_cluster, guest_cluster, came))
        olds = []
        if s == FAR_FROM:
            far, _ = lax.optimization_barrier((far, came))
            sets = [near, far]
            olds = backlog
        running = pairs(table, flat(newest), flat(olds), [stacks[p] for p in [*newest, *olds]], sets, running)
        backlog = backlog + newest
        done = [running[3]]
        newest = coming
    rows, cols = jnp.sum(running[0], axis=1), running[1]

    incoming = lax.all_to_all(cols, ("z", "x"), 0, 0, tiled=True)
    guest_density = jnp.sum(incoming, axis=(0, 1))
    home_density = to_sibling(rows[:slots]) + to_partner(rows[slots:])

    home_ids = lax.dynamic_slice_in_dim(home_cluster, device_of(y, k) * slots, slots)
    guest_id = lax.dynamic_slice_in_dim(guest_cluster, device_of(y, k), 1)

    def members(ids):
        count = jnp.sum((home_cluster[None, :] == ids[:, None]).astype(jnp.int32), axis=1)
        count = count + jnp.sum((guest_cluster[None, :] == ids[:, None]).astype(jnp.int32), axis=1)
        return count.astype(jnp.float32)

    home_score = jnp.log(1.0 + home_density) - jnp.log(members(home_ids))[:, None]
    guest_score = jnp.log(1.0 + guest_density) - jnp.log(members(guest_id))
    return home_score.reshape(-1), guest_score


def solution(mesh):
    whole = Mesh(mesh.devices.reshape(NY, NZ, NX, NH, NK), AXES)
    placed = (P(AXES, None), P(AXES, None), P(), P(), P(AXES, None, None))
    return jax.shard_map(
        body, mesh=whole, in_specs=placed, out_specs=(P(AXES), P(AXES)), check_vma=False
    )
```

```python
import functools
import math

import jax
import jax.numpy as jnp
from jax import lax
from jax.experimental import pallas as pl
from jax.experimental.pallas import tpu as pltpu
from jax.sharding import Mesh
from jax.sharding import PartitionSpec as P

BLOCK = 256
LANES = 128
SHARPNESS = 30.0
EPSILON = 1e-06
EXP2_SCALE = SHARPNESS / math.log(2.0)
UNROLL = 6
GROUP = 4
AHEAD = 6
VMEM_MIB = 63
FAR_FROM = 3
IDS_AT = 4

NY, NZ, NX, NH, NK = 2, 8, 4, 2, 2
AXES = ("y", "z", "x", "h", "k")

SLOTS = (
    ( ((0, -1), ((0, 0),)), ((-1, 0), ((0, 0),)), ((1, 0), ((0, 0),)), ((0, 1), ((0, 0),)) ),
    ( ((-1, 0), ((-1, 0),)), ((1, 0), ((1, 0),)), ((0, -1), ((-1, 0),)), ((0, 1), ((0, 1),)) ),
    ( ((1, 0), ((0, 2),)), ((0, 1), ((2, 0),)), ((0, -1), ((2, 0),)), ((-1, 0), ((-2, 0),)) ),
    ( ((-1, 0), ((2, 1), (2, -1),)), ((0, -1), ((-3, 0), (-2, 0),)), ((1, 0), ((2, 1), (2, -1),)), ((0, 1), ((-3, 0), (-2, 0),)) ),
    ( ((1, 0), ((3, 1), (3, -1),)), ((0, 1), ((3, 1), (3, -1),)), ((-1, 0), ((0, 1), (-3, 0),)), ((0, -1), ((-3, -1), (-2, -1),)) ),
    ( ((-1, 0), ((0, 2),)), ((0, -1), ((2, -1),)), ((1, 0), ((3, 2),)) ),
)


def node(dz, dx):
    return ((dz + 3) % NZ - 3, (dx + 1) % NX - 1)


def shift(value, dz, dx):
    if dx == 0:
        return lax.ppermute(value, "z", [(i, (i + dz) % NZ) for i in range(NZ)])
    if dz == 0:
        return lax.ppermute(value, "x", [(i, (i + dx) % NX) for i in range(NX)])
    return lax.ppermute(
        value,
        ("z", "x"),
        [(z * NX + x, (z + dz) % NZ * NX + (x + dx) % NX) for z in range(NZ) for x in range(NX)],
    )


def to_sibling(value):
    return lax.ppermute(value, "k", [(0, 1), (1, 0)])


def to_partner(value):
    return lax.ppermute(value, ("y", "k"), [(0, 3), (1, 2), (2, 1), (3, 0)])


def three_terms(values):
    high = values.astype(jnp.bfloat16)
    rest = values - high.astype(jnp.float32)
    middle = rest.astype(jnp.bfloat16)
    return high, middle, (rest - middle.astype(jnp.float32)).astype(jnp.bfloat16)


def lane_sums(values):
    terms = jnp.concatenate(three_terms(values), axis=1)
    ones = jnp.ones((8, terms.shape[1]), jnp.bfloat16)
    return lax.dot_general(ones, terms, (((1,), (1,)), ((), ())), preferred_element_type=jnp.float32)[:1]


def lane_totals(values):
    terms = jnp.concatenate(three_terms(values), axis=1)
    ones = jnp.ones((terms.shape[1], LANES), jnp.bfloat16)
    return lax.dot_general(terms, ones, (((1,), (0,)), ((), ())), preferred_element_type=jnp.float32)


def squares(block):
    total = None
    for part in range(block.shape[1] // LANES):
        values = block[:, part * LANES : (part + 1) * LANES].astype(jnp.float32)
        total = values * values if total is None else total + values * values
    return total


def pair_kernel(news, olds, sizes, n_sets, first, last, table, *refs):
    arrays, refs = refs[: len(sizes)], refs[len(sizes) :]
    sets, refs = refs[:n_sets], refs[n_sets:]
    n_before = 0 if first else 3 if last else 4
    before, refs = refs[:n_before], refs[n_before:]
    rows, scale, next_turn, cols, held, blocks, columns, sums, added, listed, places, sems, set_sems = refs
    n_new, n_guest = len(news), len(news) + len(olds)
    n_set, n_each = blocks.shape[0], sets[0].shape[0]
    z, x = table[table.shape[0] - 2], table[table.shape[0] - 1]

    guest_copies, at = [], 0
    for a, (array, size) in enumerate(zip(arrays, sizes, strict=True)):
        guest_copies.append((at, pltpu.make_async_copy(array, held.at[pl.ds(at, size)], sems.at[a])))
        at += size
    def start_block(r):
        for j in range(n_sets):

            @pl.when((r >= j * n_each) & (r < (j + 1) * n_each))
            def _(j=j):
                pltpu.make_async_copy(sets[j].at[r - j * n_each], blocks.at[r], set_sems.at[r]).start()

    for at, copy in guest_copies:
        if at < n_new:
            copy.start()
    for g, (dz, dx) in enumerate([*news, *olds]):
        places[g] = lax.rem(z - dz + NZ, NZ) * NX + lax.rem(x - dx + NX, NX)

    def list_pairs(first_guest, last_guest, first_block):
        def list_block(r, count):
            own = table[NZ * NX + r]
            for g in range(first_guest, last_guest):
                listed[0, count] = r
                listed[1, count] = g
                count = count + jnp.where(table[places[g]] == own, 1, 0)
            return count

        count = lax.fori_loop(first_block, n_set, list_block, 0)
        for u in range(UNROLL):
            listed[0, count + u] = first_block
            listed[1, count + u] = first_guest
        return count

    def wait_blocks(start, stop):
        def wait_block(r, _):
            pltpu.make_async_copy(sets[0].at[0], blocks.at[r], set_sems.at[r]).wait()
            start_block(r + AHEAD)
            return 0

        lax.fori_loop(start, stop, wait_block, 0)
        return jnp.maximum(start, stop)

    def run_pairs(count, waited):
        def run_step(step, waited):
            last = jnp.minimum(step * UNROLL + UNROLL, count) - 1
            waited = wait_blocks(waited, listed[0, last] + 1)
            for u in range(UNROLL):
                at = step * UNROLL + u
                r, g = listed[0, at], listed[1, at]
                keep = jnp.where(at < count, 1.0, 0.0)
                products = lax.dot_general(
                    held[g], blocks[r], (((1,), (1,)), ((), ())), preferred_element_type=jnp.float32
                )
                across, down = scale[pl.ds(r, 1), :], columns[g]
                total = sums[g]
                for half in range(BLOCK // LANES):
                    lanes = slice(half * LANES, (half + 1) * LANES)
                    tile = jnp.exp2(products[:, lanes] * down * across[:, lanes]) * keep
                    total = total + tile
                    rows[r, :, lanes] += jnp.sum(tile.reshape(BLOCK // 8, 8, LANES), axis=0)
                sums[g] = total
            return waited

        return lax.fori_loop(0, lax.div(count + UNROLL - 1, UNROLL), run_step, waited)

    def in_groups(start, stop, task):
        size = min(GROUP, stop - start)

        @pl.loop(0, -(-(stop - start) // size))
        def _(step):
            for u in range(size):
                task(jnp.minimum(start + step * size + u, stop - 1))

    def set_column(g):
        columns[g] = 1.0 / jnp.sqrt(lane_totals(squares(held.at[g])) + EPSILON)

    def set_scale(r):
        scale[pl.ds(r, 1), :] = EXP2_SCALE / jnp.sqrt(lane_sums(squares(blocks.at[r])) + EPSILON)

    def set_col_sums(g):
        if last:
            cols[g] = lane_sums(sums[g])
        else:
            cols[places[g]] = added[places[g]] + lane_sums(sums[g])

    count = list_pairs(0, n_new, 0)
    if first:
        for out in (rows, scale, next_turn, cols):
            out[...] = jnp.zeros_like(out)
    else:
        for out, value in zip((rows, scale, next_turn, cols)[:n_before], before, strict=True):
            out[...] = value[...]
    sums[...] = jnp.zeros_like(sums)
    for at, copy in guest_copies:
        if at < n_new:
            copy.wait()
    for r in range(AHEAD):
        start_block(r)
    for at, copy in guest_copies:
        if at >= n_new:
            copy.start()
    in_groups(0, n_new, set_column)
    waited = 0
    if first or olds:
        waited = wait_blocks(0, n_set)
        in_groups(n_set - n_each, n_set, set_scale)
    waited = run_pairs(count, waited)
    if olds:
        count = list_pairs(n_new, n_guest, n_set - n_each)
        for at, copy in guest_copies:
            if at >= n_new:
                copy.wait()
        in_groups(n_new, n_guest, set_column)
        waited = run_pairs(count, waited)
    wait_blocks(waited, n_set)
    if not last:
        added[...] = cols[...]
    in_groups(0, n_guest, set_col_sums)


def pairs(table, news, olds, arrays, sets, running, last):
    n_guest, n_set = len(news) + len(olds), sum(one.shape[0] for one in sets)
    smem, vmem, hbm = (pl.BlockSpec(memory_space=m) for m in (pltpu.SMEM, pltpu.VMEM, pltpu.HBM))
    first = running is None
    tiles = (len(news) * n_set + len(olds) * sets[-1].shape[0]) // 3
    shapes = [(2 * sets[0].shape[0], 8, BLOCK), (16, BLOCK), (8, LANES), (n_guest if last else NZ * NX, 1, BLOCK)]
    return pl.pallas_call(
        functools.partial(pair_kernel, news, olds, [a.shape[0] for a in arrays], len(sets), first, last),
        in_specs=[smem] + [hbm] * (len(arrays) + len(sets)) + [vmem] * (0 if first else 3 if last else 4),
        out_specs=[vmem] * 4,
        out_shape=[jax.ShapeDtypeStruct(shape, jnp.float32) for shape in shapes],
        scratch_shapes=[
            pltpu.VMEM((n_guest, *arrays[0].shape[1:]), jnp.bfloat16),
            pltpu.VMEM((n_set, *arrays[0].shape[1:]), jnp.bfloat16),
            pltpu.VMEM((n_guest, BLOCK, LANES), jnp.float32),
            pltpu.VMEM((n_guest, BLOCK, LANES), jnp.float32),
            pltpu.VMEM(shapes[3], jnp.float32),
            pltpu.SMEM((2, n_guest * n_set + UNROLL), jnp.int32),
            pltpu.SMEM((n_guest,), jnp.int32),
            pltpu.SemaphoreType.DMA((len(arrays),)),
            pltpu.SemaphoreType.DMA((n_set,)),
        ],
        compiler_params=pltpu.CompilerParams(vmem_limit_bytes=VMEM_MIB << 20),
        cost_estimate=pl.CostEstimate(
            flops=tiles * 4 * BLOCK * BLOCK * 768, bytes_accessed=tiles * 400000, transcendentals=tiles * BLOCK * BLOCK
        ),
        name="pairs",
    )(table, *arrays, *sets, *([] if first else running[:3] if last else running))


def body(home_rows, guest_rows, home_cluster, guest_cluster, pair_mask):
    slots = home_rows.shape[0] // BLOCK
    y, z, x, h, k = (lax.axis_index(a) for a in AXES)

    def device_of(yy, kk):
        return (((yy * NZ + z) * NX + x) * NH + h) * NK + kk

    table = jnp.concatenate([
        lax.dynamic_slice(guest_cluster.reshape(NY, NZ * NX, NH * NK), (y, 0, h * NK + k), (1, NZ * NX, 1)).reshape(-1),
        lax.dynamic_slice_in_dim(home_cluster, device_of(y, 1 - k) * slots, slots),
        lax.dynamic_slice_in_dim(home_cluster, device_of(1 - y, 1 - k) * slots, slots),
        jnp.stack([z, x]),
    ])

    stacks = {((0, 0),): guest_rows[None]}

    def one(n):
        for nodes, blocks in stacks.items():
            if n in nodes:
                return blocks[nodes.index(n)]
        raise ValueError(n)

    def send(slot, after):
        sends = [(stacks[p] if p in stacks else jnp.stack([one(n) for n in p]), p, d) for d, p in slot]
        blocks, _ = lax.optimization_barrier((tuple(b for b, _, _ in sends), tuple(after)))
        made = []
        for block, (_, parents, (dz, dx)) in zip(blocks, sends, strict=True):
            made.append(tuple(node(n[0] + dz, n[1] + dx) for n in parents))
            stacks[made[-1]] = shift(block, dz, dx)
        return made

    def flat(groups):
        return [n for nodes in groups for n in nodes]

    far = to_partner(home_rows).reshape(slots, BLOCK, -1)
    near = to_sibling(home_rows).reshape(slots, BLOCK, -1)
    newest = [((0, 0),), *send(SLOTS[0][:3], []), *send(SLOTS[0][3:], [near])]
    sets, running = [near], None
    backlog, done = [], [table]
    for s in range(1, len(SLOTS) + 1):
        came = tuple(stacks[p] for p in newest)
        coming = send(SLOTS[s], [*came, *done]) if s < len(SLOTS) else []
        if s == IDS_AT:
            home_cluster, guest_cluster, _ = lax.optimization_barrier((home_cluster, guest_cluster, came))
        olds = []
        if s == FAR_FROM:
            far, _ = lax.optimization_barrier((far, came))
            sets = [near, far]
            olds = backlog
        last = s == len(SLOTS)
        if last:
            incoming = lax.all_to_all(running[3], ("z", "x"), 0, 0, tiled=True)
        running = pairs(table, flat(newest), flat(olds), [stacks[p] for p in [*newest, *olds]], sets, running, last)
        if last:
            incoming, _ = lax.optimization_barrier((incoming, running[3]))
            late = [shift(running[3][i], -dz, -dx) for i, (dz, dx) in enumerate(flat(newest))]
        backlog = backlog + newest
        done = [running[2]]
        newest = coming
    rows = jnp.sum(running[0], axis=1)

    guest_density = jnp.sum(incoming, axis=(0, 1)) + sum(part[0] for part in late)
    home_density = to_sibling(rows[:slots]) + to_partner(rows[slots:])

    home_ids = lax.dynamic_slice_in_dim(home_cluster, device_of(y, k) * slots, slots)
    guest_id = lax.dynamic_slice_in_dim(guest_cluster, device_of(y, k), 1)

    def members(ids):
        count = jnp.sum((home_cluster[None, :] == ids[:, None]).astype(jnp.int32), axis=1)
        count = count + jnp.sum((guest_cluster[None, :] == ids[:, None]).astype(jnp.int32), axis=1)
        return count.astype(jnp.float32)

    home_score = jnp.log(1.0 + home_density) - jnp.log(members(home_ids))[:, None]
    guest_score = jnp.log(1.0 + guest_density) - jnp.log(members(guest_id))
    return home_score.reshape(-1), guest_score


def solution(mesh):
    whole = Mesh(mesh.devices.reshape(NY, NZ, NX, NH, NK), AXES)
    placed = (P(AXES, None), P(AXES, None), P(), P(), P(AXES, None, None))
    return jax.shard_map(
        body, mesh=whole, in_specs=placed, out_specs=(P(AXES), P(AXES)), check_vma=False
    )
```

```python
import functools
import math

import jax
import jax.numpy as jnp
from jax import lax
from jax.experimental import pallas as pl
from jax.experimental.pallas import tpu as pltpu
from jax.sharding import Mesh
from jax.sharding import PartitionSpec as P

BLOCK = 256
LANES = 128
SHARPNESS = 30.0
EPSILON = 1e-06
EXP2_SCALE = SHARPNESS / math.log(2.0)
UNROLL = 6
GROUP = 4
AHEAD = 6
VMEM_MIB = 63
FAR_FROM = 3
IDS_AT = 4

NY, NZ, NX, NH, NK = 2, 8, 4, 2, 2
AXES = ("y", "z", "x", "h", "k")

SLOTS = (
    ( ((0, -1), ((0, 0),)), ((-1, 0), ((0, 0),)), ((1, 0), ((0, 0),)), ((0, 1), ((0, 0),)) ),
    ( ((-1, 0), ((-1, 0),)), ((1, 0), ((1, 0),)), ((0, -1), ((-1, 0),)), ((0, 1), ((0, 1),)) ),
    ( ((1, 0), ((0, 2),)), ((0, 1), ((2, 0),)), ((0, -1), ((2, 0),)), ((-1, 0), ((-2, 0),)) ),
    ( ((-1, 0), ((2, 1), (2, -1),)), ((0, -1), ((-3, 0), (-2, 0),)), ((1, 0), ((2, 1), (2, -1),)), ((0, 1), ((-3, 0), (-2, 0),)) ),
    ( ((1, 0), ((3, 1), (3, -1),)), ((0, 1), ((3, 1), (3, -1),)), ((-1, 0), ((0, 1), (-3, 0),)), ((0, -1), ((-3, -1), (-2, -1),)) ),
    ( ((-1, 0), ((0, 2),)), ((0, -1), ((2, -1),)), ((1, 0), ((3, 2),)) ),
)


def node(dz, dx):
    return ((dz + 3) % NZ - 3, (dx + 1) % NX - 1)


def shift(value, dz, dx):
    if dx == 0:
        return lax.ppermute(value, "z", [(i, (i + dz) % NZ) for i in range(NZ)])
    if dz == 0:
        return lax.ppermute(value, "x", [(i, (i + dx) % NX) for i in range(NX)])
    return lax.ppermute(
        value,
        ("z", "x"),
        [(z * NX + x, (z + dz) % NZ * NX + (x + dx) % NX) for z in range(NZ) for x in range(NX)],
    )


def to_sibling(value):
    return lax.ppermute(value, "k", [(0, 1), (1, 0)])


def to_partner(value):
    return lax.ppermute(value, ("y", "k"), [(0, 3), (1, 2), (2, 1), (3, 0)])


def three_terms(values):
    high = values.astype(jnp.bfloat16)
    rest = values - high.astype(jnp.float32)
    middle = rest.astype(jnp.bfloat16)
    return high, middle, (rest - middle.astype(jnp.float32)).astype(jnp.bfloat16)


def lane_sums(values):
    terms = jnp.concatenate(three_terms(values), axis=1)
    ones = jnp.ones((8, terms.shape[1]), jnp.bfloat16)
    return lax.dot_general(ones, terms, (((1,), (1,)), ((), ())), preferred_element_type=jnp.float32)[:1]


def lane_totals(values):
    terms = jnp.concatenate(three_terms(values), axis=1)
    ones = jnp.ones((terms.shape[1], LANES), jnp.bfloat16)
    return lax.dot_general(terms, ones, (((1,), (0,)), ((), ())), preferred_element_type=jnp.float32)


def squares(block):
    total = None
    for part in range(block.shape[1] // LANES):
        values = block[:, part * LANES : (part + 1) * LANES].astype(jnp.float32)
        total = values * values if total is None else total + values * values
    return total


def pair_kernel(news, olds, sizes, n_sets, first, last, table, *refs):
    arrays, refs = refs[: len(sizes)], refs[len(sizes) :]
    sets, refs = refs[:n_sets], refs[n_sets:]
    n_before = 0 if first else 3 if last else 4
    before, refs = refs[:n_before], refs[n_before:]
    rows, scale, next_turn, cols, held, blocks, columns, sums, added, listed, places, sems, set_sems = refs
    n_new, n_guest = len(news), len(news) + len(olds)
    n_set, n_each = blocks.shape[0], sets[0].shape[0]
    z, x = table[table.shape[0] - 2], table[table.shape[0] - 1]

    guest_copies, at = [], 0
    for a, (array, size) in enumerate(zip(arrays, sizes, strict=True)):
        guest_copies.append((at, pltpu.make_async_copy(array, held.at[pl.ds(at, size)], sems.at[a])))
        at += size
    def start_block(r):
        for j in range(n_sets):

            @pl.when((r >= j * n_each) & (r < (j + 1) * n_each))
            def _(j=j):
                pltpu.make_async_copy(sets[j].at[r - j * n_each], blocks.at[r], set_sems.at[r]).start()

    for at, copy in guest_copies:
        if at < n_new:
            copy.start()
    for g, (dz, dx) in enumerate([*news, *olds]):
        places[g] = lax.rem(z - dz + NZ, NZ) * NX + lax.rem(x - dx + NX, NX)

    def list_pairs(first_guest, last_guest, first_block):
        def list_block(r, count):
            own = table[NZ * NX + r]
            for g in range(first_guest, last_guest):
                listed[0, count] = r
                listed[1, count] = g
                count = count + jnp.where(table[places[g]] == own, 1, 0)
            return count

        count = lax.fori_loop(first_block, n_set, list_block, 0)
        for u in range(UNROLL):
            listed[0, count + u] = first_block
            listed[1, count + u] = first_guest
        return count

    def wait_blocks(start, stop):
        def wait_block(r, _):
            pltpu.make_async_copy(sets[0].at[0], blocks.at[r], set_sems.at[r]).wait()
            start_block(r + AHEAD)
            return 0

        lax.fori_loop(start, stop, wait_block, 0)
        return jnp.maximum(start, stop)

    def run_pairs(count, waited):
        def run_step(step, waited):
            last = jnp.minimum(step * UNROLL + UNROLL, count) - 1
            waited = wait_blocks(waited, listed[0, last] + 1)
            for u in range(UNROLL):
                at = step * UNROLL + u
                r, g = listed[0, at], listed[1, at]
                keep = jnp.where(at < count, 1.0, 0.0)
                products = lax.dot_general(
                    held[g], blocks[r], (((1,), (1,)), ((), ())), preferred_element_type=jnp.float32
                )
                across, down = scale[pl.ds(r, 1), :], columns[g]
                total = sums[g]
                for half in range(BLOCK // LANES):
                    lanes = slice(half * LANES, (half + 1) * LANES)
                    tile = jnp.exp2(products[:, lanes] * down * across[:, lanes]) * keep
                    total = total + tile
                    rows[r, :, lanes] += jnp.sum(tile.reshape(BLOCK // 8, 8, LANES), axis=0)
                sums[g] = total
            return waited

        return lax.fori_loop(0, lax.div(count + UNROLL - 1, UNROLL), run_step, waited)

    def in_groups(start, stop, task):
        size = min(GROUP, stop - start)

        @pl.loop(0, -(-(stop - start) // size))
        def _(step):
            for u in range(size):
                task(jnp.minimum(start + step * size + u, stop - 1))

    def set_column(g):
        columns[g] = 1.0 / jnp.sqrt(lane_totals(squares(held.at[g])) + EPSILON)

    def set_scale(r):
        scale[pl.ds(r, 1), :] = EXP2_SCALE / jnp.sqrt(lane_sums(squares(blocks.at[r])) + EPSILON)

    def set_col_sums(g):
        if last:
            cols[g] = lane_sums(sums[g])
        else:
            cols[places[g]] = added[places[g]] + lane_sums(sums[g])

    count = list_pairs(0, n_new, 0)
    if first:
        for out in (rows, scale, next_turn, cols):
            out[...] = jnp.zeros_like(out)
    else:
        for out, value in zip((rows, scale, next_turn, cols)[:n_before], before, strict=True):
            out[...] = value[...]
    sums[...] = jnp.zeros_like(sums)
    for at, copy in guest_copies:
        if at < n_new:
            copy.wait()
    for r in range(AHEAD):
        start_block(r)
    for at, copy in guest_copies:
        if at >= n_new:
            copy.start()
    in_groups(0, n_new, set_column)
    waited = 0
    if first or olds:
        waited = wait_blocks(0, n_set)
        in_groups(n_set - n_each, n_set, set_scale)
    waited = run_pairs(count, waited)
    if olds:
        count = list_pairs(n_new, n_guest, n_set - n_each)
        for at, copy in guest_copies:
            if at >= n_new:
                copy.wait()
        in_groups(n_new, n_guest, set_column)
        waited = run_pairs(count, waited)
    wait_blocks(waited, n_set)
    if not last:
        added[...] = cols[...]
    in_groups(0, n_guest, set_col_sums)


def pairs(table, news, olds, arrays, sets, running, last):
    n_guest, n_set = len(news) + len(olds), sum(one.shape[0] for one in sets)
    smem, vmem, hbm = (pl.BlockSpec(memory_space=m) for m in (pltpu.SMEM, pltpu.VMEM, pltpu.HBM))
    first = running is None
    tiles = (len(news) * n_set + len(olds) * sets[-1].shape[0]) // 3
    shapes = [(2 * sets[0].shape[0], 8, BLOCK), (16, BLOCK), (8, LANES), (n_guest if last else NZ * NX, 1, BLOCK)]
    return pl.pallas_call(
        functools.partial(pair_kernel, news, olds, [a.shape[0] for a in arrays], len(sets), first, last),
        in_specs=[smem] + [hbm] * (len(arrays) + len(sets)) + [vmem] * (0 if first else 3 if last else 4),
        out_specs=[vmem] * 4,
        out_shape=[jax.ShapeDtypeStruct(shape, jnp.float32) for shape in shapes],
        scratch_shapes=[
            pltpu.VMEM((n_guest, *arrays[0].shape[1:]), jnp.bfloat16),
            pltpu.VMEM((n_set, *arrays[0].shape[1:]), jnp.bfloat16),
            pltpu.VMEM((n_guest, BLOCK, LANES), jnp.float32),
            pltpu.VMEM((n_guest, BLOCK, LANES), jnp.float32),
            pltpu.VMEM(shapes[3], jnp.float32),
            pltpu.SMEM((2, n_guest * n_set + UNROLL), jnp.int32),
            pltpu.SMEM((n_guest,), jnp.int32),
            pltpu.SemaphoreType.DMA((len(arrays),)),
            pltpu.SemaphoreType.DMA((n_set,)),
        ],
        compiler_params=pltpu.CompilerParams(vmem_limit_bytes=VMEM_MIB << 20),
        cost_estimate=pl.CostEstimate(
            flops=tiles * 4 * BLOCK * BLOCK * 768, bytes_accessed=tiles * 400000, transcendentals=tiles * BLOCK * BLOCK
        ),
        name="pairs",
    )(table, *arrays, *sets, *([] if first else running[:3] if last else running))


def body(home_rows, guest_rows, home_cluster, guest_cluster, pair_mask):
    slots = home_rows.shape[0] // BLOCK
    y, z, x, h, k = (lax.axis_index(a) for a in AXES)

    def device_of(yy, kk):
        return (((yy * NZ + z) * NX + x) * NH + h) * NK + kk

    table = jnp.concatenate([
        lax.dynamic_slice(guest_cluster.reshape(NY, NZ * NX, NH * NK), (y, 0, h * NK + k), (1, NZ * NX, 1)).reshape(-1),
        lax.dynamic_slice_in_dim(home_cluster, device_of(y, 1 - k) * slots, slots),
        lax.dynamic_slice_in_dim(home_cluster, device_of(1 - y, 1 - k) * slots, slots),
        jnp.stack([z, x]),
    ])

    stacks = {((0, 0),): guest_rows[None]}

    def one(n):
        for nodes, blocks in stacks.items():
            if n in nodes:
                return blocks[nodes.index(n)]
        raise ValueError(n)

    def send(slot, after):
        sends = [(stacks[p] if p in stacks else jnp.stack([one(n) for n in p]), p, d) for d, p in slot]
        blocks, _ = lax.optimization_barrier((tuple(b for b, _, _ in sends), tuple(after)))
        made = []
        for block, (_, parents, (dz, dx)) in zip(blocks, sends, strict=True):
            made.append(tuple(node(n[0] + dz, n[1] + dx) for n in parents))
            stacks[made[-1]] = shift(block, dz, dx)
        return made

    def flat(groups):
        return [n for nodes in groups for n in nodes]

    far = to_partner(home_rows).reshape(slots, BLOCK, -1)
    near = to_sibling(home_rows).reshape(slots, BLOCK, -1)
    newest = [((0, 0),), *send(SLOTS[0][:3], []), *send(SLOTS[0][3:], [near])]
    sets, running = [near], None
    backlog, done = [], [table]
    for s in range(1, len(SLOTS) + 1):
        came = tuple(stacks[p] for p in newest)
        coming = send(SLOTS[s], [*came, *done]) if s < len(SLOTS) else []
        olds = []
        if s == FAR_FROM:
            far, _ = lax.optimization_barrier((far, came))
            sets = [near, far]
            olds = backlog
        last = s == len(SLOTS)
        if last:
            incoming = lax.all_to_all(running[3], ("z", "x"), 0, 0, tiled=True)
        running = pairs(table, flat(newest), flat(olds), [stacks[p] for p in [*newest, *olds]], sets, running, last)
        if last:
            incoming, _ = lax.optimization_barrier((incoming, running[3]))
            late = [shift(running[3][i], -dz, -dx) for i, (dz, dx) in enumerate(flat(newest))]
        backlog = backlog + newest
        done = [running[2]]
        if s == IDS_AT:
            home_cluster, guest_cluster, _ = lax.optimization_barrier((home_cluster, guest_cluster, running[2]))
        newest = coming
    rows = jnp.sum(running[0], axis=1)

    guest_density = jnp.sum(incoming, axis=(0, 1)) + sum(part[0] for part in late)
    home_density = to_sibling(rows[:slots]) + to_partner(rows[slots:])

    home_ids = lax.dynamic_slice_in_dim(home_cluster, device_of(y, k) * slots, slots)
    guest_id = lax.dynamic_slice_in_dim(guest_cluster, device_of(y, k), 1)

    def members(ids):
        count = jnp.sum((home_cluster[None, :] == ids[:, None]).astype(jnp.int32), axis=1)
        count = count + jnp.sum((guest_cluster[None, :] == ids[:, None]).astype(jnp.int32), axis=1)
        return count.astype(jnp.float32)

    home_score = jnp.log(1.0 + home_density) - jnp.log(members(home_ids))[:, None]
    guest_score = jnp.log(1.0 + guest_density) - jnp.log(members(guest_id))
    return home_score.reshape(-1), guest_score


def solution(mesh):
    whole = Mesh(mesh.devices.reshape(NY, NZ, NX, NH, NK), AXES)
    placed = (P(AXES, None), P(AXES, None), P(), P(), P(AXES, None, None))
    return jax.shard_map(
        body, mesh=whole, in_specs=placed, out_specs=(P(AXES), P(AXES)), check_vma=False
    )
```
